512 devices in a mesh: rowpt: 32 (over y, z_hi, core), colpt: 16 (over z_lo, x).
Axes of the slice: x: 4, y: 4, z: 16 (z_hi: 4, z_lo: 4; z = z_hi * 4 + z_lo), core: 2. Of those that a mesh axis runs over, the one named last changes fastest.
Arguments:
- x_pairs: float32 [4, 1024, 1024], P(None, 'rowpt', 'colpt'), may hold values from -6 to 6
- eps_val: float32 [1024], P('rowpt'), may hold values from -2 to -0.5
- eps_con: float32 [1024], P('colpt'), may hold values from 0.5 to 2
- orb_val: float32 [8192, 1024], P(('rowpt', 'colpt')), may hold values from -0.35 to 0.35
- orb_con: float32 [8192, 1024], P(('rowpt', 'colpt')), may hold values from -0.35 to 0.35
- screened_w: float32 [8192, 8192], P('rowpt', 'colpt'), may hold values from -0.0625 to 0.0625
Outputs:
- hx: float32 [4, 1024, 1024], P(None, 'rowpt', 'colpt')
The draws below stay inside these ranges and needn't reach their ends.
All inputs are finite; a program needn't handle non-finite values.
Results may differ from the reference program's by a relative error of at most 0.00005.
Values sent between devices are 32-bit elements; how exact they have to be, the bound alone decides.
A program may use at most 64 MiB of HBM per device.

```python
import jax
import jax.numpy as jnp
from jax import lax

NV = 1024
NC = 1024
NP = 8192
B = 4


def level_of(rng, extent, split, least, top_value):
    factor_of, own = 1.0, jax.random.fold_in(rng, 6)
    for axis_at, shards_of in split:
        draws = jnp.exp(jax.random.uniform(jax.random.fold_in(own, axis_at), (shards_of,), jnp.float32, least / len(split), top_value / len(split)))
        factor_of = factor_of * jnp.repeat(draws, extent[axis_at] // shards_of).reshape([-1 if axis == axis_at else 1 for axis in range(len(extent))])
    return factor_of


def scatter_about(rng, dims, width, most, split=(), dtype=jnp.bfloat16):
    result = jax.random.normal(rng, dims, jnp.float32) * width
    if len(split) > 0:
        result = level_of(rng, dims, split, -0.22, 0.18) * result
    return jnp.clip(result, min=-most, max=most).astype(dtype)


def setup_inputs(seed: int = 0) -> dict:
    arg_keys = jax.random.split(jax.random.key(seed), 7)
    x_pairs = scatter_about(arg_keys[0], (B, NV, NC), 1.0, 6.0, ((1, 32), (2, 16)), jnp.float32)
    eps_val = jnp.clip(-2.0 + 1.5 * jax.random.uniform(arg_keys[1], (NV,), jnp.float32) ** level_of(arg_keys[1], (NV,), ((0, 32),), -0.2, 0.2), -2.0, -0.5)
    eps_con = jnp.clip(0.5 + 1.5 * jax.random.uniform(arg_keys[2], (NC,), jnp.float32) ** level_of(arg_keys[2], (NC,), ((0, 16),), -0.2, 0.2), 0.5, 2.0)
    orb_val = scatter_about(arg_keys[3], (NP, NV), 0.053, 0.35, ((0, 512),), jnp.float32)
    orb_con = scatter_about(arg_keys[4], (NP, NC), 0.053, 0.35, ((0, 512),), jnp.float32)
    screened_w = scatter_about(arg_keys[5], (NP, NP), NP ** -0.5, 0.0625, ((0, 32), (1, 16)), jnp.float32)
    return {"x_pairs": x_pairs, "eps_val": eps_val, "eps_con": eps_con, "orb_val": orb_val, "orb_con": orb_con, "screened_w": screened_w}


def reference(x_pairs, eps_val, eps_con, orb_val, orb_con, screened_w):
    def density_one(x_one):
        through = jnp.dot(orb_con, x_one.T, precision=lax.Precision.HIGHEST)
        return jnp.sum(through * orb_val, axis=1)

    density = lax.map(density_one, x_pairs)
    screened = jnp.dot(density, screened_w.T, precision=lax.Precision.HIGHEST)

    def kernel_one(pot_one):
        weighted = orb_val * pot_one[:, None]
        return jnp.dot(weighted.T, orb_con, precision=lax.Precision.HIGHEST)

    kernel = lax.map(kernel_one, screened)
    diff = eps_con[None, None, :] - eps_val[None, :, None]
    return diff * x_pairs + kernel
```

```python
import jax
import jax.numpy as jnp
from jax import lax
from jax.experimental import pallas as pl
from jax.experimental.pallas import tpu as pltpu
from jax.sharding import PartitionSpec as P

MESH = pl.DeviceIdType.MESH
F32 = jnp.float32
BF16 = jnp.bfloat16

V1, C1, V2, C2, XD, DA, DB, DW, SA, SB, KD = range(11)
NSEM = 11


def halves(a):
    hi = a.astype(BF16)
    return hi, (a - hi.astype(F32)).astype(BF16)


def dot_of(a, b, dims):
    return lax.dot_general(a, b, (dims, ((), ())), preferred_element_type=F32)


def dot3(a, b, dims):
    (ah, al), (bh, bl) = a, b
    return dot_of(ah, bh, dims) + (dot_of(ah, bl, dims) + dot_of(al, bh, dims))


NT = ((1,), (1,))
NN = ((1,), (0,))


def kernel(
    x_ref, val_ref, con_ref, w_ref, out_ref,
    xp, xr, v1, c1, vb, cb, vt, ch, cl, wh, wl,
    dpart, da, das, db, dbs, dw, sp, sa, sas, sb, kp, kr,
    rsem, ssem, selfsem,
):
    row = lax.axis_index("rowpt")
    col = lax.axis_index("colpt")
    y, zh, k = row // 8, (row // 2) % 4, row % 2
    zl, x = col // 4, col % 4
    s, h = zl % 2, zl // 2

    def row_of(y_, zh_, k_):
        return y_ * 8 + zh_ * 2 + k_

    def send(src, dst, sem, to_row, to_col):
        pltpu.make_async_remote_copy(
            src_ref=src, dst_ref=dst, send_sem=ssem.at[sem], recv_sem=rsem.at[sem],
            device_id=(to_row, to_col), device_id_type=MESH,
        ).start()

    def keep(src, dst, sem):
        pltpu.make_async_copy(src, dst, rsem.at[sem]).start()

    def arrived(buf, sem):
        pltpu.make_async_copy(buf, buf, rsem.at[sem]).wait()

    def sent(buf, sem):
        pltpu.make_async_copy(buf, buf, ssem.at[sem]).wait()

    def cols(block, width):
        return pl.ds(pl.multiple_of(block * width, width), width)

    for d in range(1, 4):
        to = (y + d) % 4
        send(val_ref.at[:, cols(to, 256)], v1.at[y], V1, row_of(to, zh, k), col)
        to = (x + d) % 4
        send(con_ref.at[:, cols(to, 256)], c1.at[x], C1, row, zl * 4 + to)
    keep(val_ref.at[:, cols(y, 256)], v1.at[y], V1)
    keep(con_ref.at[:, cols(x, 256)], c1.at[x], C1)

    xp[...] = jnp.concatenate([x_ref[:, 0:16, :], x_ref[:, 16:32, :]], axis=2)
    xslot = (zh % 2) * 4 + k * 2 + x % 2
    for a in range(4):
        for b in range(2):
            to_row = row_of(y, (zh + a) % 4, x // 2)
            to_col = (((h + b) % 2) * 2 + zh // 2) * 4 + zl
            if a or b:
                send(xp, xr.at[xslot], XD, to_row, to_col)
            else:
                xself = (to_row == row) & (to_col == col)

                @pl.when(xself)
                def _():
                    keep(xp, xr.at[xslot], XD)

                @pl.when(jnp.logical_not(xself))
                def _():
                    pltpu.make_async_remote_copy(
                        src_ref=xp, dst_ref=xr.at[xslot], send_sem=selfsem.at[0], recv_sem=rsem.at[XD],
                        device_id=(to_row, to_col), device_id_type=MESH,
                    ).start()

    arrived(v1, V1)
    for d in range(1, 16):
        to_x, to_s, to_k = (x + d // 4) % 4, (s + d // 2) % 2, (k + d) % 2
        send(v1.at[:, :, cols(to_s, 128)], vb.at[:, k, s, x], V2, row_of(y, zh, to_k), (h * 2 + to_s) * 4 + to_x)
    keep(v1.at[:, :, cols(s, 128)], vb.at[:, k, s, x], V2)
    arrived(c1, C1)
    for d in range(1, 16):
        to_y, to_s, to_k = (y + d // 4) % 4, (s + d // 2) % 2, (k + d) % 2
        send(c1.at[:, :, cols(to_k, 128)], cb.at[y, k, s], C2, row_of(to_y, zh, to_k), (h * 2 + to_s) * 4 + x)
    keep(c1.at[:, :, cols(k, 128)], cb.at[y, k, s], C2)

    w_hi, w_lo = halves(w_ref[...])
    wh[...] = w_hi
    wl[...] = w_lo

    arrived(xr, XD)
    lane = lax.broadcasted_iota(jnp.int32, (4, 16, 128), 2)
    parts = []
    for v in range(4):
        one, two = xr[v * 2], xr[v * 2 + 1]
        parts.append(jnp.where(lane < 64, one, pltpu.roll(two, 64, 2)))
        parts.append(jnp.where(lane < 64, pltpu.roll(one, 64, 2), two))
    trial = jnp.concatenate([p[:, None] for p in parts], axis=1).reshape(512, 128)
    trial = halves(trial)
    arrived(cb, C2)
    arrived(vb, V2)
    for blk in range(4):
        c_hi, c_lo = halves(cb[blk].reshape(256, 128))
        ch[blk] = c_hi
        cl[blk] = c_lo
        v_t = vb[blk].reshape(256, 128).T
        vt[blk] = v_t
        through = dot3(trial, (c_hi, c_lo), NT).reshape(4, 128, 256)
        dens = jnp.sum(through * v_t[None], axis=1)
        dpart[blk] = jnp.concatenate([dens[:, :128], dens[:, 128:]], axis=0)

    for d in range(1, 8):
        to_x, to_k = (x + d // 2) % 4, (k + d) % 2
        send(dpart.at[to_x], da.at[x * 2 + k], DA, row_of(y, zh, to_k), zl * 4 + to_x)
    keep(dpart.at[x], da.at[x * 2 + k], DA)
    arrived(da, DA)
    das[...] = jnp.sum(da[...], axis=0)
    for d in range(1, 8):
        to_y, to_s = (y + d // 2) % 4, (s + d) % 2
        send(das, db.at[y * 2 + s], DB, row_of(to_y, zh, k), (h * 2 + to_s) * 4 + x)
    keep(das, db.at[y * 2 + s], DB)
    arrived(db, DB)
    dbs[...] = jnp.sum(db[...], axis=0)

    dselves = []
    for e in range(2):
        to_row = row_of(y, s * 2 + e, k)
        to_col = x * 4 + zh
        dself = (to_row == row) & (to_col == col)
        dselves.append(dself)

        @pl.when(dself)
        def _():
            keep(dbs, dw.at[h], DW)

        @pl.when(jnp.logical_not(dself))
        def _():
            pltpu.make_async_remote_copy(
                src_ref=dbs, dst_ref=dw.at[h], send_sem=selfsem.at[1 + e], recv_sem=rsem.at[DW],
                device_id=(to_row, to_col), device_id_type=MESH,
            ).start()
    arrived(dw, DW)
    d0, d1 = dw[0], dw[1]
    dens = jnp.concatenate([d0[0:4], d1[0:4], d0[4:8], d1[4:8]], axis=1)
    dens = jnp.concatenate([dens, dens], axis=0)
    scr = dot3(halves(dens), (wh[...], wl[...]), NT)
    sp[...] = jnp.concatenate([scr[0:4, :128], scr[0:4, 128:]], axis=0)

    for d in range(1, 16):
        send(sp, sa.at[col], SA, row, (col + d) % 16)
    keep(sp, sa.at[col], SA)
    arrived(sa, SA)
    sas[...] = jnp.sum(sa[...], axis=0)
    for d in range(1, 8):
        to_y, to_k = (y + d // 2) % 4, (k + d) % 2
        send(sas, sb.at[y * 2 + k], SB, row_of(to_y, zh, to_k), col)
    keep(sas, sb.at[y * 2 + k], SB)
    arrived(sb, SB)

    acc = jnp.zeros((512, 128), F32)
    for blk in range(4):
        pots = []
        for kk in range(2):
            tile = sb[blk * 2 + kk]
            pots.append(jnp.where(h == 0, tile[0:4], tile[4:8]))
        pot = jnp.concatenate(pots, axis=1)
        weighted = (vt[blk][None] * pot[:, None, :]).reshape(512, 256)
        acc = acc + dot3(halves(weighted), (ch[blk], cl[blk]), NN)
    acc = acc.reshape(4, 8, 16, 128)
    for v in range(4):
        one, two = acc[:, v * 2], acc[:, v * 2 + 1]
        kp[v * 2] = jnp.where(lane < 64, one, pltpu.roll(two, 64, 2))
        kp[v * 2 + 1] = jnp.where(lane < 64, pltpu.roll(one, 64, 2), two)

    group = zh * 2 + h
    for e in range(8):
        slot = (xslot + e) % 8
        to_row = row_of(y, s * 2 + slot // 4, (slot // 2) % 2)
        to_col = x * 4 + k * 2 + slot % 2
        if e:
            send(kp.at[slot], kr.at[group], KD, to_row, to_col)
        else:
            kself = (to_row == row) & (to_col == col)

            @pl.when(kself)
            def _():
                keep(kp.at[slot], kr.at[group], KD)

            @pl.when(jnp.logical_not(kself))
            def _():
                pltpu.make_async_remote_copy(
                    src_ref=kp.at[slot], dst_ref=kr.at[group], send_sem=selfsem.at[3], recv_sem=rsem.at[KD],
                    device_id=(to_row, to_col), device_id_type=MESH,
                ).start()
    arrived(kr, KD)
    total = jnp.sum(kr[...], axis=0)
    out_ref[:, 0:16, :] = total[:, :, :64]
    out_ref[:, 16:32, :] = total[:, :, 64:]

    sent(v1.at[0:3], V1)
    sent(c1.at[0:3], C1)
    sent(vt.at[:, 0:120], V2)
    sent(vt.at[:, 0:120], C2)
    sent(xr.at[0:7], XD)
    sent(da.at[0:7], DA)
    sent(db.at[0:7], DB)
    sent(sa.at[0:15], SA)
    sent(sb.at[0:7], SB)
    sent(kr.at[0:7], KD)

    @pl.when(jnp.logical_not(xself))
    def _():
        pltpu.make_async_copy(xp, xp, selfsem.at[0]).wait()

    for e in range(2):

        @pl.when(jnp.logical_not(dselves[e]))
        def _():
            pltpu.make_async_copy(dbs, dbs, selfsem.at[1 + e]).wait()

    @pl.when(jnp.logical_not(kself))
    def _():
        pltpu.make_async_copy(kr.at[0], kr.at[0], selfsem.at[3]).wait()


def per_device(x_pairs, eps_val, eps_con, orb_val, orb_con, screened_w):
    vmem = pl.BlockSpec(memory_space=pltpu.VMEM)
    kern = pl.pallas_call(
        kernel,
        out_shape=jax.ShapeDtypeStruct((4, 32, 64), F32),
        in_specs=[vmem] * 4,
        out_specs=vmem,
        scratch_shapes=[
            pltpu.VMEM((4, 16, 128), F32),
            pltpu.VMEM((8, 4, 16, 128), F32),
            pltpu.VMEM((4, 16, 256), F32),
            pltpu.VMEM((4, 16, 256), F32),
            pltpu.VMEM((4, 2, 2, 4, 16, 128), F32),
            pltpu.VMEM((4, 2, 2, 4, 16, 128), F32),
            pltpu.VMEM((4, 128, 256), F32),
            pltpu.VMEM((4, 256, 128), BF16),
            pltpu.VMEM((4, 256, 128), BF16),
            pltpu.VMEM((256, 512), BF16),
            pltpu.VMEM((256, 512), BF16),
            pltpu.VMEM((4, 8, 128), F32),
            pltpu.VMEM((8, 8, 128), F32),
            pltpu.VMEM((8, 128), F32),
            pltpu.VMEM((8, 8, 128), F32),
            pltpu.VMEM((8, 128), F32),
            pltpu.VMEM((2, 8, 128), F32),
            pltpu.VMEM((8, 128), F32),
            pltpu.VMEM((16, 8, 128), F32),
            pltpu.VMEM((8, 128), F32),
            pltpu.VMEM((8, 8, 128), F32),
            pltpu.VMEM((8, 4, 16, 128), F32),
            pltpu.VMEM((8, 4, 16, 128), F32),
            pltpu.SemaphoreType.DMA((NSEM,)),
            pltpu.SemaphoreType.DMA((NSEM,)),
            pltpu.SemaphoreType.DMA((4,)),
        ],
        compiler_params=pltpu.CompilerParams(has_side_effects=True),
        name="bse_apply",
    )(x_pairs, orb_val, orb_con, screened_w)
    diff = eps_con[None, None, :] - eps_val[None, :, None]
    return diff * x_pairs + kern


def solution(mesh):
    in_specs = (
        P(None, "rowpt", "colpt"),
        P("rowpt"),
        P("colpt"),
        P(("rowpt", "colpt"), None),
        P(("rowpt", "colpt"), None),
        P("rowpt", "colpt"),
    )
    out_specs = P(None, "rowpt", "colpt")
    return jax.shard_map(
        per_device, mesh=mesh, in_specs=in_specs, out_specs=out_specs, check_vma=False
    )
```

```python
import jax
import jax.numpy as jnp
from jax import lax
from jax.experimental import pallas as pl
from jax.experimental.pallas import tpu as pltpu
from jax.sharding import PartitionSpec as P

MESH = pl.DeviceIdType.MESH
F32 = jnp.float32
BF16 = jnp.bfloat16

V1, C1, CZ, V2, C2, DA, DB, DW, SA, SB, KD = range(11)
NSEM = 11


def halves(a):
    hi = a.astype(BF16)
    return hi, (a - hi.astype(F32)).astype(BF16)


def dot_of(a, b, dims):
    return lax.dot_general(a, b, (dims, ((), ())), preferred_element_type=F32)


def dot3(a, b, dims):
    (ah, al), (bh, bl) = a, b
    return dot_of(ah, bh, dims) + (dot_of(ah, bl, dims) + dot_of(al, bh, dims))


NT = ((1,), (1,))
NN = ((1,), (0,))


def kernel(
    x_ref, val_ref, con_ref, w_ref, out_ref,
    xp, xr, v1, c1, vb, cb, vt, ch, cl, wh, wl,
    dpart, da, das, db, dbs, dw, sp, sa, sas, sb, kp, kr,
    rsem, ssem, selfsem, xsem, xout,
):
    row = lax.axis_index("rowpt")
    col = lax.axis_index("colpt")
    y, zh, k = row // 8, (row // 2) % 4, row % 2
    zl, x = col // 4, col % 4
    s, h = zl % 2, zl // 2

    def row_of(y_, zh_, k_):
        return y_ * 8 + zh_ * 2 + k_

    def send(src, dst, sem, to_row, to_col):
        pltpu.make_async_remote_copy(
            src_ref=src, dst_ref=dst, send_sem=ssem.at[sem], recv_sem=rsem.at[sem],
            device_id=(to_row, to_col), device_id_type=MESH,
        ).start()

    def keep(src, dst, sem):
        pltpu.make_async_copy(src, dst, rsem.at[sem]).start()

    def arrived(buf, sem):
        pltpu.make_async_copy(buf, buf, rsem.at[sem]).wait()

    leaving = []

    def sent(buf, sem, only=None):
        def wait():
            pltpu.make_async_copy(buf, buf, sem).wait()

        leaving.append(wait if only is None else lambda: pl.when(only)(wait))

    def cols(block, width):
        return pl.ds(pl.multiple_of(block * width, width), width)

    def send_or_keep(src, dst, sem, own_sem, to):
        same = (to[0] == row) & (to[1] == col)

        @pl.when(same)
        def _():
            pltpu.make_async_copy(src, dst, sem).start()

        @pl.when(jnp.logical_not(same))
        def _():
            pltpu.make_async_remote_copy(
                src_ref=src, dst_ref=dst, send_sem=own_sem, recv_sem=sem,
                device_id=to, device_id_type=MESH,
            ).start()

        sent(src, own_sem, jnp.logical_not(same))

    xslot = (zh % 2) * 4 + k * 2 + x % 2

    def ring_peer(d):
        to = (zh * 2 + h + d) % 8
        return row_of(y, to // 2, k), ((to % 2) * 2 + s) * 4 + x

    def pair_peer(slot):
        return row_of(y, s * 2 + slot // 4, (slot // 2) % 2), x * 4 + k * 2 + slot % 2

    def density_peer(e):
        return row_of(y, s * 2 + e, k), x * 4 + zh

    near = []
    for d in range(1, 16):
        near.append((row_of(y, zh, (k + d) % 2), (h * 2 + (s + d // 2) % 2) * 4 + (x + d // 4) % 4))
    for d in range(4, 16):
        near.append((row_of((y + d // 4) % 4, zh, (k + d) % 2), (h * 2 + (s + d // 2) % 2) * 4 + x))
    for d in range(8):
        near.append((row, ((1 - h) * 2 + d // 4) * 4 + d % 4))
    near += [ring_peer(1), ring_peer(-1)]
    barrier = pltpu.get_barrier_semaphore()
    for to in near:
        pl.semaphore_signal(barrier, inc=1, device_id=to, device_id_type=MESH)
    pl.semaphore_wait(barrier, len(near))

    xp[...] = jnp.concatenate([x_ref[:, 0:16, :], x_ref[:, 16:32, :]], axis=2)
    send_or_keep(
        xp, xr.at[xslot], xsem.at[xslot], selfsem.at[0],
        (row_of(y, zh, x // 2), (h * 2 + zh // 2) * 4 + zl),
    )

    def way_of(q):
        return (zh * 2 + h - 4 * s - 2 * q - x // 2 + 16) % 8

    def hand_on(q):
        way = way_of(q)
        for j in range(4):
            piece = xr.at[q * 4 + j]
            pltpu.make_async_copy(piece, piece, xsem.at[q * 4 + j]).wait()
            for on, going in enumerate((way <= 3, (way == 0) | (way >= 6))):
                out = xout.at[on, q * 4 + j]

                @pl.when(going)
                def _():
                    pltpu.make_async_remote_copy(
                        src_ref=piece, dst_ref=piece, send_sem=out, recv_sem=xsem.at[q * 4 + j],
                        device_id=ring_peer(1 - 2 * on), device_id_type=MESH,
                    ).start()

    for q in range(2):
        for on, going in enumerate((way_of(q) <= 3, (way_of(q) == 0) | (way_of(q) >= 6))):
            for j in range(4):
                sent(xp, xout.at[on, q * 4 + j], going)

    def steps_of(q):
        way = way_of(q)
        return jnp.minimum(way, 8 - way)

    first = jnp.where(steps_of(0) <= steps_of(1), 0, 1)
    at_start = way_of(first) == 0

    for d in range(1, 8):
        to_x, to_k = (x + d // 2) % 4, (k + d) % 2
        send(con_ref.at[:, cols(to_x * 2 + to_k, 128)], c1.at[k, x], C1, row_of(y, zh, to_k), zl * 4 + to_x)
    keep(con_ref.at[:, cols(x * 2 + k, 128)], c1.at[k, x], C1)
    for d in range(1, 8):
        to_y, to_s = (y + d // 2) % 4, (s + d) % 2
        send(val_ref.at[:, cols(to_y * 2 + to_s, 128)], v1.at[y, s], V1, row_of(to_y, zh, k), (h * 2 + to_s) * 4 + x)
    keep(val_ref.at[:, cols(y * 2 + s, 128)], v1.at[y, s], V1)
    sent(xr.at[0:7, 0], ssem.at[C1])
    sent(xr.at[0:7, 0], ssem.at[V1])

    pl.when(at_start)(lambda: hand_on(first))

    partner = (h * 2 + 1 - s) * 4 + x
    arrived(c1, C1)
    send(c1, cb.at[y, :, s], CZ, row, partner)
    keep(c1, cb.at[y, :, s], C2)
    for d in range(1, 4):
        send(c1, cb.at[y, :, s], C2, row_of((y + d) % 4, zh, k), col)
    arrived(v1, V1)
    for d in range(1, 8):
        to_x, to_k = (x + d // 2) % 4, (k + d) % 2
        send(v1, vb.at[:, k, :, x], V2, row_of(y, zh, to_k), zl * 4 + to_x)
    keep(v1, vb.at[:, k, :, x], V2)
    pl.when(jnp.logical_not(at_start))(lambda: hand_on(first))
    arrived(c1, CZ)
    for d in range(1, 4):
        send(cb.at[y, :, 1 - s], cb.at[y, :, 1 - s], C2, row_of((y + d) % 4, zh, k), col)
    hand_on(1 - first)
    sent(c1, ssem.at[CZ])
    sent(vt.at[:, 0:96], ssem.at[C2])
    sent(vt.at[:, 0:112], ssem.at[V2])

    w_hi, w_lo = halves(w_ref[...])
    wh[...] = w_hi
    wl[...] = w_lo

    lane = lax.broadcasted_iota(jnp.int32, (4, 16, 128), 2)
    parts = []
    for v in range(4):
        one, two = xr[v * 2], xr[v * 2 + 1]
        parts.append(jnp.where(lane < 64, one, pltpu.roll(two, 64, 2)))
        parts.append(jnp.where(lane < 64, pltpu.roll(one, 64, 2), two))
    trial = jnp.concatenate([p[:, None] for p in parts], axis=1).reshape(512, 128)
    trial = halves(trial)
    arrived(vt.at[:, 0:112], C2)
    arrived(vb, V2)
    for blk in range(4):
        c_hi, c_lo = halves(cb[blk].reshape(256, 128))
        ch[blk] = c_hi
        cl[blk] = c_lo
        v_t = vb[blk].reshape(256, 128).T
        vt[blk] = v_t
        through = dot3(trial, (c_hi, c_lo), NT).reshape(4, 128, 256)
        dens = jnp.sum(through * v_t[None], axis=1)
        dpart[blk] = jnp.concatenate([dens[:, :128], dens[:, 128:]], axis=0)

    for d in range(1, 8):
        to_x, to_k = (x + d // 2) % 4, (k + d) % 2
        send(dpart.at[to_x], da.at[x * 2 + k], DA, row_of(y, zh, to_k), zl * 4 + to_x)
    keep(dpart.at[x], da.at[x * 2 + k], DA)
    sent(da.at[0:7], ssem.at[DA])
    arrived(da, DA)
    das[...] = jnp.sum(da[...], axis=0)
    for d in range(1, 8):
        to_y, to_s = (y + d // 2) % 4, (s + d) % 2
        send(das, db.at[y * 2 + s], DB, row_of(to_y, zh, k), (h * 2 + to_s) * 4 + x)
    keep(das, db.at[y * 2 + s], DB)
    sent(db.at[0:7], ssem.at[DB])
    arrived(db, DB)
    dbs[...] = jnp.sum(db[...], axis=0)

    for e in range(2):
        send_or_keep(dbs, dw.at[h], rsem.at[DW], selfsem.at[1 + e], density_peer(e))
    arrived(dw, DW)
    d0, d1 = dw[0], dw[1]
    dens = jnp.concatenate([d0[0:4], d1[0:4], d0[4:8], d1[4:8]], axis=1)
    dens = jnp.concatenate([dens, dens], axis=0)
    scr = dot3(halves(dens), (wh[...], wl[...]), NT)
    sp[...] = jnp.concatenate([scr[0:4, :128], scr[0:4, 128:]], axis=0)

    for d in range(1, 16):
        send(sp, sa.at[col], SA, row, (col + d) % 16)
    keep(sp, sa.at[col], SA)
    sent(sa.at[0:15], ssem.at[SA])
    arrived(sa, SA)
    sas[...] = jnp.sum(sa[...], axis=0)
    for d in range(1, 8):
        to_y, to_k = (y + d // 2) % 4, (k + d) % 2
        send(sas, sb.at[y * 2 + k], SB, row_of(to_y, zh, to_k), col)
    keep(sas, sb.at[y * 2 + k], SB)
    sent(sb.at[0:7], ssem.at[SB])
    arrived(sb, SB)

    acc = jnp.zeros((512, 128), F32)
    for blk in range(4):
        pots = []
        for kk in range(2):
            tile = sb[blk * 2 + kk]
            pots.append(jnp.where(h == 0, tile[0:4], tile[4:8]))
        pot = jnp.concatenate(pots, axis=1)
        weighted = (vt[blk][None] * pot[:, None, :]).reshape(512, 256)
        acc = acc + dot3(halves(weighted), (ch[blk], cl[blk]), NN)
    acc = acc.reshape(4, 8, 16, 128)
    for v in range(4):
        one, two = acc[:, v * 2], acc[:, v * 2 + 1]
        kp[v * 2] = jnp.where(lane < 64, one, pltpu.roll(two, 64, 2))
        kp[v * 2 + 1] = jnp.where(lane < 64, pltpu.roll(one, 64, 2), two)

    away = (s * 8 + x - zh * 4 - zl + 33) % 16
    far = jnp.where(away < 7, 1, 0)
    group = zh * 2 + h
    for half in (far, 1 - far):
        for j in (1, 2, 3, 0):
            slot = half * 4 + (k * 2 + x % 2 + j) % 4
            to = pair_peer(slot)
            if half is far or j:
                send(kp.at[slot], kr.at[group], KD, *to)
            else:
                send_or_keep(kp.at[slot], kr.at[group], rsem.at[KD], selfsem.at[3], to)
    sent(kr.at[0:7], ssem.at[KD])
    arrived(kr, KD)
    total = jnp.sum(kr[...], axis=0)
    out_ref[:, 0:16, :] = total[:, :, :64]
    out_ref[:, 16:32, :] = total[:, :, 64:]

    for wait in leaving:
        wait()


def per_device(x_pairs, eps_val, eps_con, orb_val, orb_con, screened_w):
    vmem = pl.BlockSpec(memory_space=pltpu.VMEM)
    kern = pl.pallas_call(
        kernel,
        out_shape=jax.ShapeDtypeStruct((4, 32, 64), F32),
        in_specs=[vmem] * 4,
        out_specs=vmem,
        scratch_shapes=[
            pltpu.VMEM((4, 16, 128), F32),
            pltpu.VMEM((8, 4, 16, 128), F32),
            pltpu.VMEM((4, 2, 16, 128), F32),
            pltpu.VMEM((2, 4, 16, 128), F32),
            pltpu.VMEM((4, 2, 2, 4, 16, 128), F32),
            pltpu.VMEM((4, 2, 2, 4, 16, 128), F32),
            pltpu.VMEM((4, 128, 256), F32),
            pltpu.VMEM((4, 256, 128), BF16),
            pltpu.VMEM((4, 256, 128), BF16),
            pltpu.VMEM((256, 512), BF16),
            pltpu.VMEM((256, 512), BF16),
            pltpu.VMEM((4, 8, 128), F32),
            pltpu.VMEM((8, 8, 128), F32),
            pltpu.VMEM((8, 128), F32),
            pltpu.VMEM((8, 8, 128), F32),
            pltpu.VMEM((8, 128), F32),
            pltpu.VMEM((2, 8, 128), F32),
            pltpu.VMEM((8, 128), F32),
            pltpu.VMEM((16, 8, 128), F32),
            pltpu.VMEM((8, 128), F32),
            pltpu.VMEM((8, 8, 128), F32),
            pltpu.VMEM((8, 4, 16, 128), F32),
            pltpu.VMEM((8, 4, 16, 128), F32),
            pltpu.SemaphoreType.DMA((NSEM,)),
            pltpu.SemaphoreType.DMA((NSEM,)),
            pltpu.SemaphoreType.DMA((4,)),
            pltpu.SemaphoreType.DMA((8,)),
            pltpu.SemaphoreType.DMA((2, 8)),
        ],
        compiler_params=pltpu.CompilerParams(has_side_effects=True, collective_id=0),
        name="bse_apply",
    )(x_pairs, orb_val, orb_con, screened_w)
    diff = eps_con[None, None, :] - eps_val[None, :, None]
    return diff * x_pairs + kern


def solution(mesh):
    in_specs = (
        P(None, "rowpt", "colpt"),
        P("rowpt"),
        P("colpt"),
        P(("rowpt", "colpt"), None),
        P(("rowpt", "colpt"), None),
        P("rowpt", "colpt"),
    )
    out_specs = P(None, "rowpt", "colpt")
    return jax.shard_map(
        per_device, mesh=mesh, in_specs=in_specs, out_specs=out_specs, check_vma=False
    )
```

```python
import jax
import jax.numpy as jnp
from jax import lax
from jax.experimental import pallas as pl
from jax.experimental.pallas import tpu as pltpu
from jax.sharding import PartitionSpec as P

MESH = pl.DeviceIdType.MESH
F32 = jnp.float32
BF16 = jnp.bfloat16

V1, C1, V2, C2, V3, C3, V4, C4, DA, DB, DW, SA, SB, KD = range(14)
NSEM = 14


def halves(a):
    hi = a.astype(BF16)
    return hi, (a - hi.astype(F32)).astype(BF16)


def dot_of(a, b, dims):
    return lax.dot_general(a, b, (dims, ((), ())), preferred_element_type=F32)


def dot3(a, b, dims):
    (ah, al), (bh, bl) = a, b
    return dot_of(ah, bh, dims) + (dot_of(ah, bl, dims) + dot_of(al, bh, dims))


NT = ((1,), (1,))
NN = ((1,), (0,))


def kernel(
    x_ref, ev_ref, ec_ref, val_ref, con_ref, w_ref, out_ref,
    xv, wv, xp, xr, vb, cb, vb2, cb2, vt, ch, cl, wh, wl,
    dpart, da, das, db, dbs, dw, sp, sa, sas, sb, kp, kr,
    rsem, ssem, selfsem, xsem, xout, lsem, ready,
):
    row = lax.axis_index("rowpt")
    col = lax.axis_index("colpt")
    y, zh, k = row // 8, (row // 2) % 4, row % 2
    zl, x = col // 4, col % 4
    s, h = zl % 2, zl // 2

    def row_of(y_, zh_, k_):
        return y_ * 8 + zh_ * 2 + k_

    def send(src, dst, sem, to_row, to_col):
        pltpu.make_async_remote_copy(
            src_ref=src, dst_ref=dst, send_sem=ssem.at[sem], recv_sem=rsem.at[sem],
            device_id=(to_row, to_col), device_id_type=MESH,
        ).start()

    def keep(src, dst, sem):
        pltpu.make_async_copy(src, dst, rsem.at[sem]).start()

    def arrived(buf, sem):
        pltpu.make_async_copy(buf, buf, rsem.at[sem]).wait()

    leaving = []

    def sent(buf, sem, only=None):
        def wait():
            pltpu.make_async_copy(buf, buf, sem).wait()

        leaving.append(wait if only is None else lambda: pl.when(only)(wait))

    def cols(block, width):
        return pl.ds(pl.multiple_of(block * width, width), width)

    def send_or_keep(src, dst, sem, own_sem, to):
        same = (to[0] == row) & (to[1] == col)

        @pl.when(same)
        def _():
            pltpu.make_async_copy(src, dst, sem).start()

        @pl.when(jnp.logical_not(same))
        def _():
            pltpu.make_async_remote_copy(
                src_ref=src, dst_ref=dst, send_sem=own_sem, recv_sem=sem,
                device_id=to, device_id_type=MESH,
            ).start()

        sent(src, own_sem, jnp.logical_not(same))

    xslot = (zh % 2) * 4 + k * 2 + x % 2

    def ring_peer(d):
        to = (zh * 2 + h + d) % 8
        return row_of(y, to // 2, k), ((to % 2) * 2 + s) * 4 + x

    def pair_peer(slot):
        return row_of(y, s * 2 + slot // 4, (slot // 2) % 2), x * 4 + k * 2 + slot % 2

    def density_peer(e):
        return row_of(y, s * 2 + e, k), x * 4 + zh

    def group_peer(d):
        to = (zh * 2 + h + d) % 8
        return row_of(y, to // 2, x // 2), ((to % 2) * 2 + zh // 2) * 4 + zl

    def way_of(q):
        return (zh * 2 + h - 4 * s - 2 * q - x // 2 + 16) % 8

    near = []
    for d in range(1, 16):
        near.append((row_of(y, zh, (k + d) % 2), (h * 2 + (s + d // 2) % 2) * 4 + (x + d // 4) % 4))
    for d in range(4, 16):
        near.append((row_of((y + d // 4) % 4, zh, (k + d) % 2), (h * 2 + (s + d // 2) % 2) * 4 + x))
    for d in range(16):
        near.append((row_of(y, zh, d // 8), ((1 - h) * 2 + d // 4 % 2) * 4 + d % 4))
    for d in range(2, 8):
        near.append((row_of((y + d // 2) % 4, zh, k), ((1 - h) * 2 + d % 2) * 4 + x))
    near += [ring_peer(1), ring_peer(-1)]
    barrier = pltpu.get_barrier_semaphore()
    for to in near:
        pl.semaphore_signal(barrier, inc=1, device_id=to, device_id_type=MESH)

    loads = [
        pltpu.make_async_copy(x_ref, xv, lsem.at[0]),
        pltpu.make_async_copy(w_ref, wv, lsem.at[1]),
    ]
    for load in loads:
        load.start()
    pl.semaphore_wait(barrier, len(near))

    def ring_ready(n):
        for d in (1, -1):
            pl.semaphore_signal(ready.at[n], inc=1, device_id=ring_peer(d), device_id_type=MESH)

    ring_ready(0)

    for d in range(1, 16):
        to_x, to_s, to_k = (x + d // 4) % 4, (s + d // 2) % 2, (k + d) % 2
        send(
            con_ref.at[:, cols(to_x * 2 + to_k, 128)], cb.at[y, k, s, x], C1,
            row_of(y, zh, to_k), (h * 2 + to_s) * 4 + to_x,
        )
    keep(con_ref.at[:, cols(x * 2 + k, 128)], cb.at[y, k, s, x], C1)
    for d in range(1, 8):
        to_y, to_s = (y + d // 2) % 4, (s + d) % 2
        send(
            val_ref.at[:, cols(to_y * 2 + to_s, 128)], vb.at[y, k, s, x], V1,
            row_of(to_y, zh, k), (h * 2 + to_s) * 4 + x,
        )
    keep(val_ref.at[:, cols(y * 2 + s, 128)], vb.at[y, k, s, x], V1)
    sent(vt.at[0, 0:120], ssem.at[C1])
    sent(xr.at[0:7, 0], ssem.at[V1])

    loads[0].wait()
    xp[...] = jnp.concatenate([xv[:, 0:16, :], xv[:, 16:32, :]], axis=2)
    pl.semaphore_wait(ready.at[0], 2)
    ring_ready(1)

    pl.semaphore_wait(ready.at[1], 2)
    for on, d in enumerate((2, -2, 1, -1)):
        pltpu.make_async_remote_copy(
            src_ref=xp, dst_ref=xr.at[xslot], send_sem=xout.at[0, on], recv_sem=xsem.at[xslot],
            device_id=group_peer(d), device_id_type=MESH,
        ).start()
        sent(xp, xout.at[0, on])
    send_or_keep(xp, xr.at[xslot], xsem.at[xslot], selfsem.at[0], group_peer(0))

    arrived(cb.at[y], C1)
    for d in (2, 1, 3):
        send(cb.at[y], cb.at[y], C2, row_of((y + d) % 4, zh, k), col)
    mine = vb.at[:, k, :, x]
    arrived(mine, V1)
    for d in (4, 5, 2, 3, 6, 7, 1):
        to_x, to_k = (x + d // 2) % 4, (k + d) % 2
        send(mine, mine, V2, row_of(y, zh, to_k), zl * 4 + to_x)
    sent(cb.at[0:3], ssem.at[C2])
    sent(vt.at[0:4, 0:112], ssem.at[V2])

    def piece_in(slot):
        pltpu.make_async_copy(xr.at[slot], xr.at[slot], xsem.at[slot]).wait()

    relays = way_of(0) % 2 == 0
    half = jnp.where(way_of(0) % 4 == 2, 0, 1)
    ahead = way_of(half) == 2
    step = jnp.where(ahead, 1, -1)
    odd = jnp.where(ahead, 0, 1)

    @pl.when(relays)
    def _():
        for n in range(4):
            slot = half * 4 + (n % 2) * 2 + (odd if n < 2 else 1 - odd)
            piece_in(slot)
            for on, to in enumerate((2 * step, step)):
                if on or n < 2:
                    pltpu.make_async_remote_copy(
                        src_ref=xr.at[slot], dst_ref=xr.at[slot], send_sem=xout.at[1 + on, n],
                        recv_sem=xsem.at[slot], device_id=ring_peer(to), device_id_type=MESH,
                    ).start()

    for on in range(2):
        for n in range(4):
            if on or n < 2:
                sent(xp, xout.at[1 + on, n], relays)

    @pl.when(jnp.logical_not(relays))
    def _():
        for n in range(4):
            piece_in(half * 4 + n)

    loads[1].wait()
    w_hi, w_lo = halves(wv[...])
    wh[...] = w_hi
    wl[...] = w_lo

    for n in range(4):
        piece_in((1 - half) * 4 + n)

    for d in range(16):
        to_x, to_s, to_k = (x + d // 4) % 4, d // 2 % 2, d % 2
        send(
            con_ref.at[:, cols(to_x * 2 + to_k, 128)], cb2.at[y, k, s, x], C3,
            row_of(y, zh, to_k), ((1 - h) * 2 + to_s) * 4 + to_x,
        )
    for d in range(8):
        to_y, to_s = (y + d // 2) % 4, d % 2
        send(
            val_ref.at[:, cols(to_y * 2 + to_s, 128)], vb2.at[y, k, s, x], V3,
            row_of(to_y, zh, k), ((1 - h) * 2 + to_s) * 4 + x,
        )
    sent(cb2.at[0], ssem.at[C3])
    sent(vb2.at[0, 0], ssem.at[V3])

    lane = lax.broadcasted_iota(jnp.int32, (4, 16, 128), 2)
    parts = []
    for v in range(4):
        one, two = xr[v * 2], xr[v * 2 + 1]
        parts.append(jnp.where(lane < 64, one, pltpu.roll(two, 64, 2)))
        parts.append(jnp.where(lane < 64, pltpu.roll(one, 64, 2), two))
    trial = jnp.concatenate([p[:, None] for p in parts], axis=1).reshape(512, 128)
    trial = halves(trial)
    arrived(cb.at[0:3], C2)
    arrived(vt.at[0:4, 0:112], V2)
    for blk in range(4):
        c_hi, c_lo = halves(cb[blk].reshape(256, 128))
        ch[blk] = c_hi
        cl[blk] = c_lo
        v_t = vb[blk].reshape(256, 128).T
        vt[blk] = v_t
        through = dot3(trial, (c_hi, c_lo), NT).reshape(4, 128, 256)
        dens = jnp.sum(through * v_t[None], axis=1)
        dpart[blk] = jnp.concatenate([dens[:, :128], dens[:, 128:]], axis=0)

    for d in range(1, 8):
        to_x, to_k = (x + d // 2) % 4, (k + d) % 2
        send(dpart.at[to_x], da.at[x * 2 + k], DA, row_of(y, zh, to_k), zl * 4 + to_x)
    keep(dpart.at[x], da.at[x * 2 + k], DA)
    sent(da.at[0:7], ssem.at[DA])
    arrived(da, DA)
    das[...] = jnp.sum(da[...], axis=0)
    for d in range(1, 8):
        to_y, to_s = (y + d // 2) % 4, (s + d) % 2
        send(das, db.at[y * 2 + s], DB, row_of(to_y, zh, k), (h * 2 + to_s) * 4 + x)
    keep(das, db.at[y * 2 + s], DB)
    sent(db.at[0:7], ssem.at[DB])
    arrived(cb2.at[y], C3)
    for d in (2, 1, 3):
        send(cb2.at[y], cb2.at[y], C4, row_of((y + d) % 4, zh, k), col)
    theirs = vb2.at[:, k, :, x]
    arrived(theirs, V3)
    for d in (4, 5, 2, 3, 6, 7, 1):
        to_x, to_k = (x + d // 2) % 4, (k + d) % 2
        send(theirs, theirs, V4, row_of(y, zh, to_k), zl * 4 + to_x)
    sent(cb2.at[0:3], ssem.at[C4])
    sent(vt.at[0:4, 0:112], ssem.at[V4])
    arrived(db, DB)
    dbs[...] = jnp.sum(db[...], axis=0)

    for e in range(2):
        send_or_keep(dbs, dw.at[h], rsem.at[DW], selfsem.at[1 + e], density_peer(e))
    arrived(dw, DW)
    d0, d1 = dw[0], dw[1]
    dens = jnp.concatenate([d0[0:4], d1[0:4], d0[4:8], d1[4:8]], axis=1)
    dens = jnp.concatenate([dens, dens], axis=0)
    scr = dot3(halves(dens), (wh[...], wl[...]), NT)
    sp[...] = jnp.concatenate([scr[0:4, :128], scr[0:4, 128:]], axis=0)

    for d in range(1, 16):
        send(sp, sa.at[col], SA, row, (col + d) % 16)
    keep(sp, sa.at[col], SA)
    sent(sa.at[0:15], ssem.at[SA])
    arrived(cb2.at[0:3], C4)
    arrived(vt.at[0:4, 0:112], V4)
    for blk in range(4):
        ch[4 + blk], cl[4 + blk] = halves(cb2[blk].reshape(256, 128))
        vt[4 + blk] = vb2[blk].reshape(256, 128).T
    arrived(sa, SA)
    sas[...] = jnp.sum(sa[...], axis=0)
    for d in range(1, 8):
        to_y, to_k = (y + d // 2) % 4, (k + d) % 2
        send(sas, sb.at[y * 2 + k], SB, row_of(to_y, zh, to_k), col)
    keep(sas, sb.at[y * 2 + k], SB)
    sent(sb.at[0:7], ssem.at[SB])
    arrived(sb, SB)

    acc = jnp.zeros((512, 128), F32)
    for blk in range(8):
        pots = []
        for kk in range(2):
            tile = sb[blk % 4 * 2 + kk]
            pots.append(jnp.where((h == 0) == (blk < 4), tile[0:4], tile[4:8]))
        pot = jnp.concatenate(pots, axis=1)
        weighted = (vt[blk][None] * pot[:, None, :]).reshape(512, 256)
        acc = acc + dot3(halves(weighted), (ch[blk], cl[blk]), NN)
    acc = acc.reshape(4, 8, 16, 128)
    for v in range(4):
        one, two = acc[:, v * 2], acc[:, v * 2 + 1]
        low = jnp.where(lane < 64, one, pltpu.roll(two, 64, 2))
        high = jnp.where(lane < 64, pltpu.roll(one, 64, 2), two)
        kp[v] = jnp.where(h == 0, low, high)

    away = (s * 8 + x - zh * 4 - zl + 33) % 16
    far = jnp.where(away < 7, 1, 0)
    for hold in (far, 1 - far):
        for j in (1, 0):
            slot = hold * 2 + (k + j) % 2
            to = pair_peer(slot * 2 + h)
            if hold is far or j:
                send(kp.at[slot], kr.at[zh], KD, *to)
            else:
                send_or_keep(kp.at[slot], kr.at[zh], rsem.at[KD], selfsem.at[3], to)
    sent(kr.at[0:3], ssem.at[KD])
    arrived(kr, KD)
    total = jnp.sum(kr[...], axis=0)
    eye = lax.broadcasted_iota(jnp.int32, (32, 32), 0) == lax.broadcasted_iota(jnp.int32, (32, 32), 1)
    ev = jnp.sum(jnp.where(eye, ev_ref[...], 0.0), axis=1, keepdims=True)
    diff = ec_ref[...] - ev
    out_ref[:, 0:16, :] = diff[None, 0:16] * xv[:, 0:16, :] + total[:, :, :64]
    out_ref[:, 16:32, :] = diff[None, 16:32] * xv[:, 16:32, :] + total[:, :, 64:]

    for wait in leaving:
        wait()


def per_device(x_pairs, eps_val, eps_con, orb_val, orb_con, screened_w):
    vmem = pl.BlockSpec(memory_space=pltpu.VMEM)
    anywhere = pl.BlockSpec(memory_space=pl.ANY)
    return pl.pallas_call(
        kernel,
        out_shape=jax.ShapeDtypeStruct((4, 32, 64), F32),
        in_specs=[anywhere, vmem, vmem, anywhere, anywhere, anywhere],
        out_specs=vmem,
        scratch_shapes=[
            pltpu.VMEM((4, 32, 64), F32),
            pltpu.VMEM((256, 512), F32),
            pltpu.VMEM((4, 16, 128), F32),
            pltpu.VMEM((8, 4, 16, 128), F32),
            pltpu.VMEM((4, 2, 2, 4, 16, 128), F32),
            pltpu.VMEM((4, 2, 2, 4, 16, 128), F32),
            pltpu.VMEM((4, 2, 2, 4, 16, 128), F32),
            pltpu.VMEM((4, 2, 2, 4, 16, 128), F32),
            pltpu.VMEM((8, 128, 256), F32),
            pltpu.VMEM((8, 256, 128), BF16),
            pltpu.VMEM((8, 256, 128), BF16),
            pltpu.VMEM((256, 512), BF16),
            pltpu.VMEM((256, 512), BF16),
            pltpu.VMEM((4, 8, 128), F32),
            pltpu.VMEM((8, 8, 128), F32),
            pltpu.VMEM((8, 128), F32),
            pltpu.VMEM((8, 8, 128), F32),
            pltpu.VMEM((8, 128), F32),
            pltpu.VMEM((2, 8, 128), F32),
            pltpu.VMEM((8, 128), F32),
            pltpu.VMEM((16, 8, 128), F32),
            pltpu.VMEM((8, 128), F32),
            pltpu.VMEM((8, 8, 128), F32),
            pltpu.VMEM((4, 4, 16, 128), F32),
            pltpu.VMEM((4, 4, 16, 128), F32),
            pltpu.SemaphoreType.DMA((NSEM,)),
            pltpu.SemaphoreType.DMA((NSEM,)),
            pltpu.SemaphoreType.DMA((4,)),
            pltpu.SemaphoreType.DMA((8,)),
            pltpu.SemaphoreType.DMA((3, 4)),
            pltpu.SemaphoreType.DMA((2,)),
            pltpu.SemaphoreType.REGULAR((2,)),
        ],
        compiler_params=pltpu.CompilerParams(has_side_effects=True, collective_id=0),
        name="bse_apply",
    )(x_pairs, eps_val[None], eps_con[None], orb_val, orb_con, screened_w)


def solution(mesh):
    in_specs = (
        P(None, "rowpt", "colpt"),
        P("rowpt"),
        P("colpt"),
        P(("rowpt", "colpt"), None),
        P(("rowpt", "colpt"), None),
        P("rowpt", "colpt"),
    )
    out_specs = P(None, "rowpt", "colpt")
    return jax.shard_map(
        per_device, mesh=mesh, in_specs=in_specs, out_specs=out_specs, check_vma=False
    )
```

```python
import jax
import jax.numpy as jnp
from jax import lax
from jax.experimental import pallas as pl
from jax.experimental.pallas import tpu as pltpu
from jax.sharding import PartitionSpec as P

MESH = pl.DeviceIdType.MESH
F32 = jnp.float32
BF16 = jnp.bfloat16

V1, C1, V2, C2, V3, C3, V4, C4, DA, DB, DW, SA, SB, KD = range(14)
NSEM = 14


def halves(a):
    hi = a.astype(BF16)
    return hi, (a - hi.astype(F32)).astype(BF16)


def dot_of(a, b, dims):
    return lax.dot_general(a, b, (dims, ((), ())), preferred_element_type=F32)


def dot3(a, b, dims):
    (ah, al), (bh, bl) = a, b
    return dot_of(ah, bh, dims) + (dot_of(ah, bl, dims) + dot_of(al, bh, dims))


NT = ((1,), (1,))
NN = ((1,), (0,))


def kernel(
    x_ref, ev_ref, ec_ref, val_ref, con_ref, w_ref, out_ref,
    xv, wv, xp, xr, vb, cb, vb2, cb2, vt, ch, cl, wh, wl,
    dpart, da, das, db, dbs, dw, sp, sa, sas, sb, kp, kr,
    rsem, ssem, selfsem, xsem, xout, lsem,
):
    row = lax.axis_index("rowpt")
    col = lax.axis_index("colpt")
    y, zh, k = row // 8, (row // 2) % 4, row % 2
    zl, x = col // 4, col % 4
    s, h = zl % 2, zl // 2

    def row_of(y_, zh_, k_):
        return y_ * 8 + zh_ * 2 + k_

    def send(src, dst, sem, to_row, to_col):
        pltpu.make_async_remote_copy(
            src_ref=src, dst_ref=dst, send_sem=ssem.at[sem], recv_sem=rsem.at[sem],
            device_id=(to_row, to_col), device_id_type=MESH,
        ).start()

    def keep(src, dst, sem):
        pltpu.make_async_copy(src, dst, rsem.at[sem]).start()

    def arrived(buf, sem):
        pltpu.make_async_copy(buf, buf, rsem.at[sem]).wait()

    leaving = []

    def sent(buf, sem, only=None):
        def wait():
            pltpu.make_async_copy(buf, buf, sem).wait()

        leaving.append(wait if only is None else lambda: pl.when(only)(wait))

    def cols(block, width):
        return pl.ds(pl.multiple_of(block * width, width), width)

    def con_cols(x_, k_):
        return cols((k_ * 2 + x_ % 2) * 2 + x_ // 2, 128)

    def send_or_keep(src, dst, sem, own_sem, to):
        same = (to[0] == row) & (to[1] == col)

        @pl.when(same)
        def _():
            pltpu.make_async_copy(src, dst, sem).start()

        @pl.when(jnp.logical_not(same))
        def _():
            pltpu.make_async_remote_copy(
                src_ref=src, dst_ref=dst, send_sem=own_sem, recv_sem=sem,
                device_id=to, device_id_type=MESH,
            ).start()

        sent(src, own_sem, jnp.logical_not(same))

    xslot = (zh % 2) * 4 + k * 2 + x % 2

    def ring_peer(d):
        to = (zh * 2 + h + d) % 8
        return row_of(y, to // 2, k), ((to % 2) * 2 + s) * 4 + x

    def pair_peer(slot):
        return row_of(y, s * 2 + slot // 4, (slot // 2) % 2), (k * 2 + x % 2) * 4 + x // 2 * 2 + slot % 2

    def density_peer(e):
        return row_of(y, s * 2 + e, k), x * 4 + zh

    def group_peer(d):
        to = (zh * 2 + h + d) % 8
        return row_of(y, to // 2, zl // 2), ((to % 2) * 2 + zh // 2) * 4 + x // 2 * 2 + zl % 2

    def way_of(q):
        return (zh * 2 + h - 4 * s - 2 * q - k + 16) % 8

    near = []
    for d in range(1, 16):
        near.append((row_of(y, zh, (k + d) % 2), (h * 2 + (s + d // 2) % 2) * 4 + (x + d // 4) % 4))
    for d in range(4, 16):
        near.append((row_of((y + d // 4) % 4, zh, (k + d) % 2), (h * 2 + (s + d // 2) % 2) * 4 + x))
    for d in range(16):
        near.append((row_of(y, zh, d // 8), ((1 - h) * 2 + d // 4 % 2) * 4 + d % 4))
    for d in range(2, 8):
        near.append((row_of((y + d // 2) % 4, zh, k), ((1 - h) * 2 + d % 2) * 4 + x))
    for d in (1, -1, 2, -2):
        near += [ring_peer(d), group_peer(d)]
    barrier = pltpu.get_barrier_semaphore()
    expected = len(near)
    for q in range(2):
        direct = jnp.where((way_of(q) + 2) % 8 < 5, 1, 0) - jnp.where(way_of(q) == 0, 1, 0)
        expected = expected + 4 * direct

        @pl.when(direct == 1)
        def _():
            for j in range(4):
                pl.semaphore_signal(barrier, inc=1, device_id=pair_peer(q * 4 + j), device_id_type=MESH)

    for to in near:
        pl.semaphore_signal(barrier, inc=1, device_id=to, device_id_type=MESH)

    loads = [
        pltpu.make_async_copy(x_ref, xv, lsem.at[0]),
        pltpu.make_async_copy(w_ref, wv, lsem.at[1]),
    ]
    for load in loads:
        load.start()
    pl.semaphore_wait(barrier, expected)


    for d in range(1, 16):
        to_x, to_s, to_k = (x + d // 4) % 4, (s + d // 2) % 2, (k + d) % 2
        send(
            con_ref.at[:, con_cols(to_x, to_k)], cb.at[y, k, s, x], C1,
            row_of(y, zh, to_k), (h * 2 + to_s) * 4 + to_x,
        )
    keep(con_ref.at[:, con_cols(x, k)], cb.at[y, k, s, x], C1)
    for d in range(1, 8):
        to_y, to_s = (y + d // 2) % 4, (s + d) % 2
        send(
            val_ref.at[:, cols(to_y * 2 + to_s, 128)], vb.at[y, k, s, x], V1,
            row_of(to_y, zh, k), (h * 2 + to_s) * 4 + x,
        )
    keep(val_ref.at[:, cols(y * 2 + s, 128)], vb.at[y, k, s, x], V1)
    sent(vt.at[0, 0:120], ssem.at[C1])
    sent(xr.at[0:7, 0], ssem.at[V1])

    loads[0].wait()
    xp[...] = jnp.concatenate([xv[:, 0:16, :], xv[:, 16:32, :]], axis=2)

    for on, d in enumerate((2, -2, 1, -1)):
        pltpu.make_async_remote_copy(
            src_ref=xp, dst_ref=xr.at[xslot], send_sem=xout.at[0, on], recv_sem=xsem.at[xslot],
            device_id=group_peer(d), device_id_type=MESH,
        ).start()
        sent(xp, xout.at[0, on])
    send_or_keep(xp, xr.at[xslot], xsem.at[xslot], selfsem.at[0], group_peer(0))

    arrived(cb.at[y], C1)
    for d in (2, 1, 3):
        send(cb.at[y], cb.at[y], C2, row_of((y + d) % 4, zh, k), col)
    mine = vb.at[:, k, :, x]
    arrived(mine, V1)
    for d in (4, 5, 2, 3, 6, 7, 1):
        to_x, to_k = (x + d // 2) % 4, (k + d) % 2
        send(mine, mine, V2, row_of(y, zh, to_k), zl * 4 + to_x)
    sent(cb.at[0:3], ssem.at[C2])
    sent(vt.at[0:4, 0:112], ssem.at[V2])

    def piece_in(slot):
        pltpu.make_async_copy(xr.at[slot], xr.at[slot], xsem.at[slot]).wait()

    relays = way_of(0) % 2 == 0
    half = jnp.where(way_of(0) % 4 == 2, 0, 1)
    ahead = way_of(half) == 2
    step = jnp.where(ahead, 1, -1)
    odd = jnp.where(ahead, 0, 1)

    @pl.when(relays)
    def _():
        for n in range(4):
            slot = half * 4 + (n % 2) * 2 + (odd if n < 2 else 1 - odd)
            piece_in(slot)
            for on, to in enumerate((2 * step, step)):
                if on or n < 2:
                    pltpu.make_async_remote_copy(
                        src_ref=xr.at[slot], dst_ref=xr.at[slot], send_sem=xout.at[1 + on, n],
                        recv_sem=xsem.at[slot], device_id=ring_peer(to), device_id_type=MESH,
                    ).start()

    for on in range(2):
        for n in range(4):
            if on or n < 2:
                sent(xp, xout.at[1 + on, n], relays)

    @pl.when(jnp.logical_not(relays))
    def _():
        for n in range(4):
            piece_in(half * 4 + n)

    loads[1].wait()
    w_hi, w_lo = halves(wv[...])
    wh[...] = w_hi
    wl[...] = w_lo

    for n in range(4):
        piece_in((1 - half) * 4 + n)

    for d in range(16):
        to_x, to_s, to_k = (x + d // 4) % 4, d // 2 % 2, d % 2
        send(
            con_ref.at[:, con_cols(to_x, to_k)], cb2.at[y, k, s, x], C3,
            row_of(y, zh, to_k), ((1 - h) * 2 + to_s) * 4 + to_x,
        )
    for d in range(8):
        to_y, to_s = (y + d // 2) % 4, d % 2
        send(
            val_ref.at[:, cols(to_y * 2 + to_s, 128)], vb2.at[y, k, s, x], V3,
            row_of(to_y, zh, k), ((1 - h) * 2 + to_s) * 4 + x,
        )
    sent(cb2.at[0], ssem.at[C3])
    sent(vb2.at[0, 0], ssem.at[V3])

    lane = lax.broadcasted_iota(jnp.int32, (4, 16, 128), 2)
    parts = []
    for v in range(4):
        one, two = xr[v * 2], xr[v * 2 + 1]
        parts.append(jnp.where(lane < 64, one, pltpu.roll(two, 64, 2)))
        parts.append(jnp.where(lane < 64, pltpu.roll(one, 64, 2), two))
    trial = jnp.concatenate([p[:, None] for p in parts], axis=1).reshape(512, 128)
    trial = halves(trial)
    arrived(cb.at[0:3], C2)
    arrived(vt.at[0:4, 0:112], V2)
    for blk in range(4):
        c_hi, c_lo = halves(cb[blk].reshape(256, 128))
        ch[blk] = c_hi
        cl[blk] = c_lo
        v_t = vb[blk].reshape(256, 128).T
        vt[blk] = v_t
        through = dot3(trial, (c_hi, c_lo), NT).reshape(4, 128, 256)
        dens = jnp.sum(through * v_t[None], axis=1)
        dpart[blk] = jnp.concatenate([dens[:, :128], dens[:, 128:]], axis=0)

    for d in range(1, 8):
        to_x, to_k = (x + d // 2) % 4, (k + d) % 2
        send(dpart.at[to_x], da.at[x * 2 + k], DA, row_of(y, zh, to_k), zl * 4 + to_x)
    keep(dpart.at[x], da.at[x * 2 + k], DA)
    sent(da.at[0:7], ssem.at[DA])
    arrived(da, DA)
    das[...] = jnp.sum(da[...], axis=0)
    for d in range(1, 8):
        to_y, to_s = (y + d // 2) % 4, (s + d) % 2
        send(das, db.at[y * 2 + s], DB, row_of(to_y, zh, k), (h * 2 + to_s) * 4 + x)
    keep(das, db.at[y * 2 + s], DB)
    sent(db.at[0:7], ssem.at[DB])
    arrived(db, DB)
    dbs[...] = jnp.sum(db[...], axis=0)

    for e in range(2):
        send_or_keep(dbs, dw.at[h], rsem.at[DW], selfsem.at[1 + e], density_peer(e))
    arrived(cb2.at[y], C3)
    for d in (2, 1, 3):
        send(cb2.at[y], cb2.at[y], C4, row_of((y + d) % 4, zh, k), col)
    theirs = vb2.at[:, k, :, x]
    arrived(theirs, V3)
    for d in (4, 5, 2, 3, 6, 7, 1):
        to_x, to_k = (x + d // 2) % 4, (k + d) % 2
        send(theirs, theirs, V4, row_of(y, zh, to_k), zl * 4 + to_x)
    sent(cb2.at[0:3], ssem.at[C4])
    sent(vt.at[0:4, 0:112], ssem.at[V4])
    arrived(dw, DW)
    d0, d1 = dw[0], dw[1]
    dens = jnp.concatenate([d0[0:4], d1[0:4], d0[4:8], d1[4:8]], axis=1)
    dens = jnp.concatenate([dens, dens], axis=0)
    scr = dot3(halves(dens), (wh[...], wl[...]), NT)
    sp[...] = jnp.concatenate([scr[0:4, :128], scr[0:4, 128:]], axis=0)

    for d in range(1, 16):
        send(sp, sa.at[col], SA, row, (col + d) % 16)
    keep(sp, sa.at[col], SA)
    sent(sa.at[0:15], ssem.at[SA])
    arrived(cb2.at[0:3], C4)
    arrived(vt.at[0:4, 0:112], V4)
    for blk in range(4):
        ch[4 + blk], cl[4 + blk] = halves(cb2[blk].reshape(256, 128))
        vt[4 + blk] = vb2[blk].reshape(256, 128).T
    arrived(sa, SA)
    sas[...] = jnp.sum(sa[...], axis=0)
    for d in range(1, 8):
        to_y, to_k = (y + d // 2) % 4, (k + d) % 2
        send(sas, sb.at[y * 2 + k], SB, row_of(to_y, zh, to_k), col)
    keep(sas, sb.at[y * 2 + k], SB)
    sent(sb.at[0:7], ssem.at[SB])
    arrived(sb, SB)

    acc = jnp.zeros((512, 128), F32)
    for blk in range(8):
        pots = []
        for kk in range(2):
            tile = sb[blk % 4 * 2 + kk]
            pots.append(jnp.where((h == 0) == (blk < 4), tile[0:4], tile[4:8]))
        pot = jnp.concatenate(pots, axis=1)
        weighted = (vt[blk][None] * pot[:, None, :]).reshape(512, 256)
        acc = acc + dot3(halves(weighted), (ch[blk], cl[blk]), NN)
    acc = acc.reshape(4, 8, 16, 128)
    for v in range(4):
        one, two = acc[:, v * 2], acc[:, v * 2 + 1]
        low = jnp.where(lane < 64, one, pltpu.roll(two, 64, 2))
        high = jnp.where(lane < 64, pltpu.roll(one, 64, 2), two)
        kp[v] = jnp.where(h == 0, low, high)

    away = (s * 8 + k * 2 + x % 2 - zh * 4 - zl + 33) % 16
    far = jnp.where(away < 7, 1, 0)
    for hold in (far, 1 - far):
        for j in (1, 0):
            slot = hold * 2 + (k + j) % 2
            to = pair_peer(slot * 2 + h)
            if hold is far or j:
                send(kp.at[slot], kr.at[zh], KD, *to)
            else:
                send_or_keep(kp.at[slot], kr.at[zh], rsem.at[KD], selfsem.at[3], to)
    sent(kr.at[0:3], ssem.at[KD])
    arrived(kr, KD)
    total = jnp.sum(kr[...], axis=0)
    eye = lax.broadcasted_iota(jnp.int32, (32, 32), 0) == lax.broadcasted_iota(jnp.int32, (32, 32), 1)
    ev = jnp.sum(jnp.where(eye, ev_ref[...], 0.0), axis=1, keepdims=True)
    diff = ec_ref[...] - ev
    out_ref[:, 0:16, :] = diff[None, 0:16] * xv[:, 0:16, :] + total[:, :, :64]
    out_ref[:, 16:32, :] = diff[None, 16:32] * xv[:, 16:32, :] + total[:, :, 64:]

    for wait in leaving:
        wait()


def per_device(x_pairs, eps_val, eps_con, orb_val, orb_con, screened_w):
    vmem = pl.BlockSpec(memory_space=pltpu.VMEM)
    anywhere = pl.BlockSpec(memory_space=pl.ANY)
    return pl.pallas_call(
        kernel,
        out_shape=jax.ShapeDtypeStruct((4, 32, 64), F32),
        in_specs=[anywhere, vmem, vmem, anywhere, anywhere, anywhere],
        out_specs=vmem,
        scratch_shapes=[
            pltpu.VMEM((4, 32, 64), F32),
            pltpu.VMEM((256, 512), F32),
            pltpu.VMEM((4, 16, 128), F32),
            pltpu.VMEM((8, 4, 16, 128), F32),
            pltpu.VMEM((4, 2, 2, 4, 16, 128), F32),
            pltpu.VMEM((4, 2, 2, 4, 16, 128), F32),
            pltpu.VMEM((4, 2, 2, 4, 16, 128), F32),
            pltpu.VMEM((4, 2, 2, 4, 16, 128), F32),
            pltpu.VMEM((8, 128, 256), F32),
            pltpu.VMEM((8, 256, 128), BF16),
            pltpu.VMEM((8, 256, 128), BF16),
            pltpu.VMEM((256, 512), BF16),
            pltpu.VMEM((256, 512), BF16),
            pltpu.VMEM((4, 8, 128), F32),
            pltpu.VMEM((8, 8, 128), F32),
            pltpu.VMEM((8, 128), F32),
            pltpu.VMEM((8, 8, 128), F32),
            pltpu.VMEM((8, 128), F32),
            pltpu.VMEM((2, 8, 128), F32),
            pltpu.VMEM((8, 128), F32),
            pltpu.VMEM((16, 8, 128), F32),
            pltpu.VMEM((8, 128), F32),
            pltpu.VMEM((8, 8, 128), F32),
            pltpu.VMEM((4, 4, 16, 128), F32),
            pltpu.VMEM((4, 4, 16, 128), F32),
            pltpu.SemaphoreType.DMA((NSEM,)),
            pltpu.SemaphoreType.DMA((NSEM,)),
            pltpu.SemaphoreType.DMA((4,)),
            pltpu.SemaphoreType.DMA((8,)),
            pltpu.SemaphoreType.DMA((3, 4)),
            pltpu.SemaphoreType.DMA((2,)),
        ],
        compiler_params=pltpu.CompilerParams(has_side_effects=True, collective_id=0),
        name="bse_apply",
    )(x_pairs, eps_val[None], eps_con[None], orb_val, orb_con, screened_w)


def solution(mesh):
    in_specs = (
        P(None, "rowpt", "colpt"),
        P("rowpt"),
        P("colpt"),
        P(("rowpt", "colpt"), None),
        P(("rowpt", "colpt"), None),
        P("rowpt", "colpt"),
    )
    out_specs = P(None, "rowpt", "colpt")
    return jax.shard_map(
        per_device, mesh=mesh, in_specs=in_specs, out_specs=out_specs, check_vma=False
    )
```

```python
import jax
import jax.numpy as jnp
from jax import lax
from jax.experimental import pallas as pl
from jax.experimental.pallas import tpu as pltpu
from jax.sharding import PartitionSpec as P

MESH = pl.DeviceIdType.MESH
F32 = jnp.float32
BF16 = jnp.bfloat16

V1, C1, V2, C2, V3, C3, V4, C4, DA, DB, DW, SA, SB, KD = range(14)
NSEM = 14


def halves(a):
    hi = a.astype(BF16)
    return hi, (a - hi.astype(F32)).astype(BF16)


def dot_of(a, b, dims):
    return lax.dot_general(a, b, (dims, ((), ())), preferred_element_type=F32)


def dot3(a, b, dims):
    (ah, al), (bh, bl) = a, b
    return dot_of(ah, bh, dims) + (dot_of(ah, bl, dims) + dot_of(al, bh, dims))


NT = ((1,), (1,))
NN = ((1,), (0,))


def kernel(
    x_ref, ev_ref, ec_ref, val_ref, con_ref, w_ref, out_ref,
    xv, wv, xp, xr, vb, cb, vb2, cb2, vt, ch, cl, wh, wl,
    dpart, da, das, db, dbs, dw, sp, sa, sas, sb, kp, kr,
    rsem, ssem, selfsem, xsem, xout, lsem, ready,
):
    row = lax.axis_index("rowpt")
    col = lax.axis_index("colpt")
    y, zh, k = row // 8, (row // 2) % 4, row % 2
    zl, x = col // 4, col % 4
    s, h = zl % 2, zl // 2

    def row_of(y_, zh_, k_):
        return y_ * 8 + zh_ * 2 + k_

    def send(src, dst, sem, to_row, to_col):
        pltpu.make_async_remote_copy(
            src_ref=src, dst_ref=dst, send_sem=ssem.at[sem], recv_sem=rsem.at[sem],
            device_id=(to_row, to_col), device_id_type=MESH,
        ).start()

    def keep(src, dst, sem):
        pltpu.make_async_copy(src, dst, rsem.at[sem]).start()

    def arrived(buf, sem):
        pltpu.make_async_copy(buf, buf, rsem.at[sem]).wait()

    leaving = []

    def sent(buf, sem, only=None):
        def wait():
            pltpu.make_async_copy(buf, buf, sem).wait()

        leaving.append(wait if only is None else lambda: pl.when(only)(wait))

    def cols(block, width):
        return pl.ds(pl.multiple_of(block * width, width), width)

    def con_cols(x_, k_):
        return cols((k_ * 2 + x_ % 2) * 2 + x_ // 2, 128)

    def send_or_keep(src, dst, sem, own_sem, to):
        same = (to[0] == row) & (to[1] == col)

        @pl.when(same)
        def _():
            pltpu.make_async_copy(src, dst, sem).start()

        @pl.when(jnp.logical_not(same))
        def _():
            pltpu.make_async_remote_copy(
                src_ref=src, dst_ref=dst, send_sem=own_sem, recv_sem=sem,
                device_id=to, device_id_type=MESH,
            ).start()

        sent(src, own_sem, jnp.logical_not(same))

    xslot = (zh % 2) * 4 + k * 2 + x % 2

    def ring_peer(d):
        to = (zh * 2 + h + d) % 8
        return row_of(y, to // 2, k), ((to % 2) * 2 + s) * 4 + x

    def pair_peer(slot):
        return row_of(y, s * 2 + slot // 4, (slot // 2) % 2), (k * 2 + x % 2) * 4 + x // 2 * 2 + slot % 2

    def density_peer(e):
        return row_of(y, s * 2 + e, k), x * 4 + zh

    def group_peer(d):
        to = (zh * 2 + h + d) % 8
        return row_of(y, to // 2, zl // 2), ((to % 2) * 2 + zh // 2) * 4 + x // 2 * 2 + zl % 2

    def way_of(q):
        return (zh * 2 + h - 4 * s - 2 * q - k + 16) % 8

    near = []
    for d in (2, -2, 1, -1):
        near += [group_peer(d), ring_peer(d)]
    for d in (8, 9, 10, 11, 4, 5, 6, 7, 12, 13, 14, 15, 1, 2, 3):
        near.append((row_of(y, zh, (k + d) % 2), (h * 2 + (s + d // 2) % 2) * 4 + (x + d // 4) % 4))
    for d in (4, 5, 2, 3, 6, 7):
        near.append((row_of((y + d // 2) % 4, zh, k), (h * 2 + (s + d) % 2) * 4 + x))
    barrier = pltpu.get_barrier_semaphore()
    expected = len(near)
    for q in range(2):
        direct = jnp.where((way_of(q) + 2) % 8 < 5, 1, 0) - jnp.where(way_of(q) == 0, 1, 0)
        expected = expected + 4 * direct

        @pl.when(direct == 1)
        def _():
            for j in range(4):
                pl.semaphore_signal(barrier, inc=1, device_id=pair_peer(q * 4 + j), device_id_type=MESH)

    for to in near:
        pl.semaphore_signal(barrier, inc=1, device_id=to, device_id_type=MESH)

    loads = [
        pltpu.make_async_copy(x_ref, xv, lsem.at[0]),
        pltpu.make_async_copy(w_ref, wv, lsem.at[1]),
    ]
    for load in loads:
        load.start()
    pl.semaphore_wait(barrier, expected)
    pl.semaphore_signal(ready.at[0], inc=1, device_id=ring_peer(1 - 2 * h), device_id_type=MESH)


    for d in range(1, 16):
        to_x, to_s, to_k = (x + d // 4) % 4, (s + d // 2) % 2, (k + d) % 2
        send(
            con_ref.at[:, con_cols(to_x, to_k)], cb.at[y, k, s, x], C1,
            row_of(y, zh, to_k), (h * 2 + to_s) * 4 + to_x,
        )
    keep(con_ref.at[:, con_cols(x, k)], cb.at[y, k, s, x], C1)
    for d in range(1, 8):
        to_y, to_s = (y + d // 2) % 4, (s + d) % 2
        send(
            val_ref.at[:, cols(to_y * 2 + to_s, 128)], vb.at[y, k, s, x], V1,
            row_of(to_y, zh, k), (h * 2 + to_s) * 4 + x,
        )
    keep(val_ref.at[:, cols(y * 2 + s, 128)], vb.at[y, k, s, x], V1)
    sent(vt.at[0, 0:120], ssem.at[C1])
    sent(xr.at[0:7, 0], ssem.at[V1])

    loads[0].wait()
    xp[...] = jnp.concatenate([xv[:, 0:16, :], xv[:, 16:32, :]], axis=2)

    for on, d in enumerate((2, -2, 1, -1)):
        pltpu.make_async_remote_copy(
            src_ref=xp, dst_ref=xr.at[xslot], send_sem=xout.at[0, on], recv_sem=xsem.at[xslot],
            device_id=group_peer(d), device_id_type=MESH,
        ).start()
        sent(xp, xout.at[0, on])
    send_or_keep(xp, xr.at[xslot], xsem.at[xslot], selfsem.at[0], group_peer(0))

    arrived(cb.at[y], C1)
    for d in (2, 1, 3):
        send(cb.at[y], cb.at[y], C2, row_of((y + d) % 4, zh, k), col)
    mine = vb.at[:, k, :, x]
    arrived(mine, V1)
    for d in (4, 5, 2, 3, 6, 7, 1):
        to_x, to_k = (x + d // 2) % 4, (k + d) % 2
        send(mine, mine, V2, row_of(y, zh, to_k), zl * 4 + to_x)
    sent(cb.at[0:3], ssem.at[C2])
    sent(vt.at[0:4, 0:112], ssem.at[V2])

    def piece_in(slot):
        pltpu.make_async_copy(xr.at[slot], xr.at[slot], xsem.at[slot]).wait()

    relays = way_of(0) % 2 == 0
    half = jnp.where(way_of(0) % 4 == 2, 0, 1)
    ahead = way_of(half) == 2
    step = jnp.where(ahead, 1, -1)
    odd = jnp.where(ahead, 0, 1)

    @pl.when(relays)
    def _():
        for n in range(4):
            slot = half * 4 + (n % 2) * 2 + (odd if n < 2 else 1 - odd)
            piece_in(slot)
            for on, to in enumerate((2 * step, step)):
                if on or n < 2:
                    pltpu.make_async_remote_copy(
                        src_ref=xr.at[slot], dst_ref=xr.at[slot], send_sem=xout.at[1 + on, n],
                        recv_sem=xsem.at[slot], device_id=ring_peer(to), device_id_type=MESH,
                    ).start()

    for on in range(2):
        for n in range(4):
            if on or n < 2:
                sent(xp, xout.at[1 + on, n], relays)

    @pl.when(jnp.logical_not(relays))
    def _():
        for n in range(4):
            piece_in(half * 4 + n)

    loads[1].wait()
    w_hi, w_lo = halves(wv[...])
    wh[...] = w_hi
    wl[...] = w_lo

    for n in range(4):
        piece_in((1 - half) * 4 + n)

    lane = lax.broadcasted_iota(jnp.int32, (4, 16, 128), 2)
    parts = []
    for v in range(4):
        one, two = xr[v * 2], xr[v * 2 + 1]
        parts.append(jnp.where(lane < 64, one, pltpu.roll(two, 64, 2)))
        parts.append(jnp.where(lane < 64, pltpu.roll(one, 64, 2), two))
    trial = jnp.concatenate([p[:, None] for p in parts], axis=1).reshape(512, 128)
    trial = halves(trial)
    arrived(cb.at[0:3], C2)
    arrived(vt.at[0:4, 0:112], V2)
    for blk in range(4):
        c_hi, c_lo = halves(cb[blk].reshape(256, 128))
        ch[blk] = c_hi
        cl[blk] = c_lo
        v_t = vb[blk].reshape(256, 128).T
        vt[blk] = v_t
        through = dot3(trial, (c_hi, c_lo), NT).reshape(4, 128, 256)
        dens = jnp.sum(through * v_t[None], axis=1)
        dpart[blk] = jnp.concatenate([dens[:, :128], dens[:, 128:]], axis=0)

    for d in (4, 5, 2, 3, 6, 7, 1):
        to_x, to_k = (x + d // 2) % 4, (k + d) % 2
        send(dpart.at[to_x], da.at[x * 2 + k], DA, row_of(y, zh, to_k), zl * 4 + to_x)
    keep(dpart.at[x], da.at[x * 2 + k], DA)
    sent(da.at[0:7], ssem.at[DA])
    pl.semaphore_wait(ready.at[0], 1)
    for d in range(16):
        to_x, to_s, to_k = (x + d // 4) % 4, d // 2 % 2, d % 2
        send(
            con_ref.at[:, con_cols(to_x, to_k)], cb2.at[y, k, s, x], C3,
            row_of(y, zh, to_k), ((1 - h) * 2 + to_s) * 4 + to_x,
        )
    for d in range(8):
        to_y, to_s = (y + d // 2) % 4, d % 2
        send(
            val_ref.at[:, cols(to_y * 2 + to_s, 128)], vb2.at[y, k, s, x], V3,
            row_of(to_y, zh, k), ((1 - h) * 2 + to_s) * 4 + x,
        )
    sent(cb2.at[0], ssem.at[C3])
    sent(vb2.at[0, 0], ssem.at[V3])
    arrived(da, DA)
    das[...] = jnp.sum(da[...], axis=0)
    for d in (4, 5, 2, 3, 6, 7, 1):
        to_y, to_s = (y + d // 2) % 4, (s + d) % 2
        send(das, db.at[y * 2 + s], DB, row_of(to_y, zh, k), (h * 2 + to_s) * 4 + x)
    keep(das, db.at[y * 2 + s], DB)
    sent(db.at[0:7], ssem.at[DB])
    arrived(db, DB)
    dbs[...] = jnp.sum(db[...], axis=0)

    for e in range(2):
        send_or_keep(dbs, dw.at[h], rsem.at[DW], selfsem.at[1 + e], density_peer(e))
    arrived(cb2.at[y], C3)
    for d in (2, 1, 3):
        send(cb2.at[y], cb2.at[y], C4, row_of((y + d) % 4, zh, k), col)
    theirs = vb2.at[:, k, :, x]
    arrived(theirs, V3)
    for d in (4, 5, 2, 3, 6, 7, 1):
        to_x, to_k = (x + d // 2) % 4, (k + d) % 2
        send(theirs, theirs, V4, row_of(y, zh, to_k), zl * 4 + to_x)
    sent(cb2.at[0:3], ssem.at[C4])
    sent(vt.at[0:4, 0:112], ssem.at[V4])
    arrived(dw, DW)
    d0, d1 = dw[0], dw[1]
    dens = jnp.concatenate([d0[0:4], d1[0:4], d0[4:8], d1[4:8]], axis=1)
    dens = jnp.concatenate([dens, dens], axis=0)
    scr = dot3(halves(dens), (wh[...], wl[...]), NT)
    sp[...] = jnp.concatenate([scr[0:4, :128], scr[0:4, 128:]], axis=0)

    for d in (10, 6, 14, 8, 9, 11, 12, 13, 4, 5, 7, 15, 2, 1, 3):
        send(sp, sa.at[col], SA, row, (col + d) % 16)
    keep(sp, sa.at[col], SA)
    sent(sa.at[0:15], ssem.at[SA])
    arrived(cb2.at[0:3], C4)
    arrived(vt.at[0:4, 0:112], V4)
    for blk in range(4):
        ch[4 + blk], cl[4 + blk] = halves(cb2[blk].reshape(256, 128))
        vt[4 + blk] = vb2[blk].reshape(256, 128).T
    arrived(sa, SA)
    sas[...] = jnp.sum(sa[...], axis=0)
    for d in (4, 5, 2, 3, 6, 7, 1):
        to_y, to_k = (y + d // 2) % 4, (k + d) % 2
        send(sas, sb.at[y * 2 + k], SB, row_of(to_y, zh, to_k), col)
    keep(sas, sb.at[y * 2 + k], SB)
    sent(sb.at[0:7], ssem.at[SB])
    arrived(sb, SB)

    away = (s * 8 + k * 2 + x % 2 - zh * 4 - zl + 33) % 16
    far = jnp.where(away < 7, 1, 0)
    pots = []
    for blk in range(8):
        tiles = (sb[blk % 4 * 2], sb[blk % 4 * 2 + 1])
        pots.append(jnp.concatenate([jnp.where((h == 0) == (blk < 4), t[0:4], t[4:8]) for t in tiles], axis=1))
    lane = lax.broadcasted_iota(jnp.int32, (4, 16, 128), 2)
    for hold in (far, 1 - far):
        acc = jnp.zeros((256, 128), F32)
        for blk in range(8):
            rows = vt[blk, pl.ds(pl.multiple_of(hold * 64, 64), 64), :]
            weighted = (rows[None] * pots[blk][:, None, :]).reshape(256, 256)
            acc = acc + dot3(halves(weighted), (ch[blk], cl[blk]), NN)
        acc = acc.reshape(4, 4, 16, 128)
        for v in range(2):
            one, two = acc[:, v * 2], acc[:, v * 2 + 1]
            low = jnp.where(lane < 64, one, pltpu.roll(two, 64, 2))
            high = jnp.where(lane < 64, pltpu.roll(one, 64, 2), two)
            kp[hold * 2 + v] = jnp.where(h == 0, low, high)
        for j in (1, 0):
            slot = hold * 2 + (k + j) % 2
            to = pair_peer(slot * 2 + h)
            if hold is far or j:
                send(kp.at[slot], kr.at[zh], KD, *to)
            else:
                send_or_keep(kp.at[slot], kr.at[zh], rsem.at[KD], selfsem.at[3], to)
    sent(kr.at[0:3], ssem.at[KD])
    arrived(kr, KD)
    total = jnp.sum(kr[...], axis=0)
    eye = lax.broadcasted_iota(jnp.int32, (32, 32), 0) == lax.broadcasted_iota(jnp.int32, (32, 32), 1)
    ev = jnp.sum(jnp.where(eye, ev_ref[...], 0.0), axis=1, keepdims=True)
    diff = ec_ref[...] - ev
    out_ref[:, 0:16, :] = diff[None, 0:16] * xv[:, 0:16, :] + total[:, :, :64]
    out_ref[:, 16:32, :] = diff[None, 16:32] * xv[:, 16:32, :] + total[:, :, 64:]

    for wait in leaving:
        wait()


def per_device(x_pairs, eps_val, eps_con, orb_val, orb_con, screened_w):
    vmem = pl.BlockSpec(memory_space=pltpu.VMEM)
    anywhere = pl.BlockSpec(memory_space=pl.ANY)
    return pl.pallas_call(
        kernel,
        out_shape=jax.ShapeDtypeStruct((4, 32, 64), F32),
        in_specs=[anywhere, vmem, vmem, anywhere, anywhere, anywhere],
        out_specs=vmem,
        scratch_shapes=[
            pltpu.VMEM((4, 32, 64), F32),
            pltpu.VMEM((256, 512), F32),
            pltpu.VMEM((4, 16, 128), F32),
            pltpu.VMEM((8, 4, 16, 128), F32),
            pltpu.VMEM((4, 2, 2, 4, 16, 128), F32),
            pltpu.VMEM((4, 2, 2, 4, 16, 128), F32),
            pltpu.VMEM((4, 2, 2, 4, 16, 128), F32),
            pltpu.VMEM((4, 2, 2, 4, 16, 128), F32),
            pltpu.VMEM((8, 128, 256), F32),
            pltpu.VMEM((8, 256, 128), BF16),
            pltpu.VMEM((8, 256, 128), BF16),
            pltpu.VMEM((256, 512), BF16),
            pltpu.VMEM((256, 512), BF16),
            pltpu.VMEM((4, 8, 128), F32),
            pltpu.VMEM((8, 8, 128), F32),
            pltpu.VMEM((8, 128), F32),
            pltpu.VMEM((8, 8, 128), F32),
            pltpu.VMEM((8, 128), F32),
            pltpu.VMEM((2, 8, 128), F32),
            pltpu.VMEM((8, 128), F32),
            pltpu.VMEM((16, 8, 128), F32),
            pltpu.VMEM((8, 128), F32),
            pltpu.VMEM((8, 8, 128), F32),
            pltpu.VMEM((4, 4, 16, 128), F32),
            pltpu.VMEM((4, 4, 16, 128), F32),
            pltpu.SemaphoreType.DMA((NSEM,)),
            pltpu.SemaphoreType.DMA((NSEM,)),
            pltpu.SemaphoreType.DMA((4,)),
            pltpu.SemaphoreType.DMA((8,)),
            pltpu.SemaphoreType.DMA((3, 4)),
            pltpu.SemaphoreType.DMA((2,)),
            pltpu.SemaphoreType.REGULAR((1,)),
        ],
        compiler_params=pltpu.CompilerParams(has_side_effects=True, collective_id=0),
        name="bse_apply",
    )(x_pairs, eps_val[None], eps_con[None], orb_val, orb_con, screened_w)


def solution(mesh):
    in_specs = (
        P(None, "rowpt", "colpt"),
        P("rowpt"),
        P("colpt"),
        P(("rowpt", "colpt"), None),
        P(("rowpt", "colpt"), None),
        P("rowpt", "colpt"),
    )
    out_specs = P(None, "rowpt", "colpt")
    return jax.shard_map(
        per_device, mesh=mesh, in_specs=in_specs, out_specs=out_specs, check_vma=False
    )
```

```python
import jax
import jax.numpy as jnp
from jax import lax
from jax.experimental import pallas as pl
from jax.experimental.pallas import tpu as pltpu
from jax.sharding import PartitionSpec as P

MESH = pl.DeviceIdType.MESH
F32 = jnp.float32
BF16 = jnp.bfloat16

V1, C1, V2, C2, V3, C3, V4, C4, C5, DA, DB, DW, SA, SB, KD = range(15)
NSEM = 15


def halves(a):
    hi = a.astype(BF16)
    return hi, (a - hi.astype(F32)).astype(BF16)


def dot_of(a, b, dims):
    return lax.dot_general(a, b, (dims, ((), ())), preferred_element_type=F32)


def dot3(a, b, dims):
    (ah, al), (bh, bl) = a, b
    return dot_of(ah, bh, dims) + (dot_of(ah, bl, dims) + dot_of(al, bh, dims))


NT = ((1,), (1,))
NN = ((1,), (0,))


def kernel(
    x_ref, ev_ref, ec_ref, val_ref, con_ref, w_ref, out_ref,
    xv, wv, xp, xr, vb, cb, vb2, cb2, vt, ch, cl, wh, wl,
    dpart, da, das, db, dbs, dw, sp, sa, sas, sb, kp, kr,
    rsem, ssem, selfsem, xsem, xout, lsem, ready,
):
    row = lax.axis_index("rowpt")
    col = lax.axis_index("colpt")
    y, zh, k = row // 8, (row // 2) % 4, row % 2
    zl, x = col // 4, col % 4
    s, h = zl % 2, zl // 2

    def row_of(y_, zh_, k_):
        return y_ * 8 + zh_ * 2 + k_

    def send(src, dst, sem, to_row, to_col):
        pltpu.make_async_remote_copy(
            src_ref=src, dst_ref=dst, send_sem=ssem.at[sem], recv_sem=rsem.at[sem],
            device_id=(to_row, to_col), device_id_type=MESH,
        ).start()

    def keep(src, dst, sem):
        pltpu.make_async_copy(src, dst, rsem.at[sem]).start()

    def arrived(buf, sem):
        pltpu.make_async_copy(buf, buf, rsem.at[sem]).wait()

    leaving = []

    def sent(buf, sem, only=None):
        def wait():
            pltpu.make_async_copy(buf, buf, sem).wait()

        leaving.append(wait if only is None else lambda: pl.when(only)(wait))

    def cols(block, width):
        return pl.ds(pl.multiple_of(block * width, width), width)

    def con_cols(x_, k_):
        return cols((k_ * 2 + x_ % 2) * 2 + x_ // 2, 128)

    def send_or_keep(src, dst, sem, own_sem, to):
        same = (to[0] == row) & (to[1] == col)

        @pl.when(same)
        def _():
            pltpu.make_async_copy(src, dst, sem).start()

        @pl.when(jnp.logical_not(same))
        def _():
            pltpu.make_async_remote_copy(
                src_ref=src, dst_ref=dst, send_sem=own_sem, recv_sem=sem,
                device_id=to, device_id_type=MESH,
            ).start()

        sent(src, own_sem, jnp.logical_not(same))

    xslot = (zh % 2) * 4 + k * 2 + x % 2

    def ring_peer(d):
        to = (zh * 2 + h + d) % 8
        return row_of(y, to // 2, k), ((to % 2) * 2 + s) * 4 + x

    def pair_peer(slot):
        return row_of(y, s * 2 + slot // 4, (slot // 2) % 2), (k * 2 + x % 2) * 4 + x // 2 * 2 + slot % 2

    def density_peer(e):
        return row_of(y, s * 2 + e, k), x * 4 + zh

    def group_peer(d):
        to = (zh * 2 + h + d) % 8
        return row_of(y, to // 2, zl // 2), ((to % 2) * 2 + zh // 2) * 4 + x // 2 * 2 + zl % 2

    def way_of(q):
        return (zh * 2 + h - 4 * s - 2 * q - k + 16) % 8

    near = []
    for d in (2, -2, 1, -1):
        near += [group_peer(d), ring_peer(d)]
    for d in (8, 9, 10, 11, 4, 5, 6, 7, 12, 13, 14, 15, 1, 2, 3):
        near.append((row_of(y, zh, (k + d) % 2), (h * 2 + (s + d // 2) % 2) * 4 + (x + d // 4) % 4))
    for d in (4, 5, 2, 3, 6, 7):
        near.append((row_of((y + d // 2) % 4, zh, k), (h * 2 + (s + d) % 2) * 4 + x))
    barrier = pltpu.get_barrier_semaphore()
    expected = len(near)
    for q in range(2):
        direct = jnp.where((way_of(q) + 2) % 8 < 5, 1, 0) - jnp.where(way_of(q) == 0, 1, 0)
        expected = expected + 4 * direct

        @pl.when(direct == 1)
        def _():
            for j in range(4):
                pl.semaphore_signal(barrier, inc=1, device_id=pair_peer(q * 4 + j), device_id_type=MESH)

    for to in near:
        pl.semaphore_signal(barrier, inc=1, device_id=to, device_id_type=MESH)

    loads = [
        pltpu.make_async_copy(x_ref, xv, lsem.at[0]),
        pltpu.make_async_copy(w_ref, wv, lsem.at[1]),
    ]
    for load in loads:
        load.start()
    pl.semaphore_wait(barrier, expected)
    pl.semaphore_signal(ready.at[0], inc=1, device_id=ring_peer(1 - 2 * h), device_id_type=MESH)


    for d in range(1, 16):
        to_x, to_s, to_k = (x + d // 4) % 4, (s + d // 2) % 2, (k + d) % 2
        send(
            con_ref.at[:, con_cols(to_x, to_k)], cb.at[y, k, s, x], C5 if d // 2 % 2 else C1,
            row_of(y, zh, to_k), (h * 2 + to_s) * 4 + to_x,
        )
    keep(con_ref.at[:, con_cols(x, k)], cb.at[y, k, s, x], C1)
    for d in range(1, 8):
        to_y, to_s = (y + d // 2) % 4, (s + d) % 2
        send(
            val_ref.at[:, cols(to_y * 2 + to_s, 128)], vb.at[y, k, s, x], V1,
            row_of(to_y, zh, k), (h * 2 + to_s) * 4 + x,
        )
    keep(val_ref.at[:, cols(y * 2 + s, 128)], vb.at[y, k, s, x], V1)
    sent(xr.at[0:7, 0], ssem.at[C1])
    sent(xr.at[0:8, 0], ssem.at[C5])
    sent(xr.at[0:7, 0], ssem.at[V1])

    loads[0].wait()
    xp[...] = jnp.concatenate([xv[:, 0:16, :], xv[:, 16:32, :]], axis=2)

    for on, d in enumerate((2, -2, 1, -1)):
        pltpu.make_async_remote_copy(
            src_ref=xp, dst_ref=xr.at[xslot], send_sem=xout.at[0, on], recv_sem=xsem.at[xslot],
            device_id=group_peer(d), device_id_type=MESH,
        ).start()
        sent(xp, xout.at[0, on])
    send_or_keep(xp, xr.at[xslot], xsem.at[xslot], selfsem.at[0], group_peer(0))

    for sem, part in ((C1, s), (C5, 1 - s)):
        arrived(cb.at[y, :, part], sem)
        for d in (2, 1, 3):
            send(cb.at[y, :, part], cb.at[y, :, part], C2, row_of((y + d) % 4, zh, k), col)
    mine = vb.at[:, k, :, x]
    arrived(mine, V1)
    for d in (4, 5, 2, 3, 6, 7, 1):
        to_x, to_k = (x + d // 2) % 4, (k + d) % 2
        send(mine, mine, V2, row_of(y, zh, to_k), zl * 4 + to_x)
    sent(cb.at[0:3], ssem.at[C2])
    sent(vt.at[0:4, 0:112], ssem.at[V2])

    def piece_in(slot):
        pltpu.make_async_copy(xr.at[slot], xr.at[slot], xsem.at[slot]).wait()

    relays = way_of(0) % 2 == 0
    half = jnp.where(way_of(0) % 4 == 2, 0, 1)
    ahead = way_of(half) == 2
    step = jnp.where(ahead, 1, -1)
    odd = jnp.where(ahead, 0, 1)

    @pl.when(relays)
    def _():
        for n in range(4):
            slot = half * 4 + (n % 2) * 2 + (odd if n < 2 else 1 - odd)
            piece_in(slot)
            for on, to in enumerate((2 * step, step)):
                if on or n < 2:
                    pltpu.make_async_remote_copy(
                        src_ref=xr.at[slot], dst_ref=xr.at[slot], send_sem=xout.at[1 + on, n],
                        recv_sem=xsem.at[slot], device_id=ring_peer(to), device_id_type=MESH,
                    ).start()

    for on in range(2):
        for n in range(4):
            if on or n < 2:
                sent(xp, xout.at[1 + on, n], relays)

    @pl.when(jnp.logical_not(relays))
    def _():
        for n in range(4):
            piece_in(half * 4 + n)

    loads[1].wait()
    w_hi, w_lo = halves(wv[...])
    wh[...] = w_hi
    wl[...] = w_lo

    for n in range(4):
        piece_in((1 - half) * 4 + n)

    lane = lax.broadcasted_iota(jnp.int32, (4, 16, 128), 2)
    parts = []
    for v in range(4):
        one, two = xr[v * 2], xr[v * 2 + 1]
        parts.append(jnp.where(lane < 64, one, pltpu.roll(two, 64, 2)))
        parts.append(jnp.where(lane < 64, pltpu.roll(one, 64, 2), two))
    trial = jnp.concatenate([p[:, None] for p in parts], axis=1).reshape(512, 128)
    trial = halves(trial)
    arrived(cb.at[0:3], C2)
    arrived(vt.at[0:4, 0:112], V2)
    for blk in range(4):
        c_hi, c_lo = halves(cb[blk].reshape(256, 128))
        ch[blk] = c_hi
        cl[blk] = c_lo
        v_t = vb[blk].reshape(256, 128).T
        vt[blk] = v_t
        through = dot3(trial, (c_hi, c_lo), NT).reshape(4, 128, 256)
        dens = jnp.sum(through * v_t[None], axis=1)
        dpart[blk] = jnp.concatenate([dens[:, :128], dens[:, 128:]], axis=0)

    for d in (4, 5, 2, 3, 6, 7, 1):
        to_x, to_k = (x + d // 2) % 4, (k + d) % 2
        send(dpart.at[to_x], da.at[x * 2 + k], DA, row_of(y, zh, to_k), zl * 4 + to_x)
    keep(dpart.at[x], da.at[x * 2 + k], DA)
    sent(da.at[0:7], ssem.at[DA])
    pl.semaphore_wait(ready.at[0], 1)
    for d in range(16):
        to_x, to_s, to_k = (x + d // 4) % 4, d // 2 % 2, d % 2
        send(
            con_ref.at[:, con_cols(to_x, to_k)], cb2.at[y, k, s, x], C3,
            row_of(y, zh, to_k), ((1 - h) * 2 + to_s) * 4 + to_x,
        )
    for d in range(8):
        to_y, to_s = (y + d // 2) % 4, d % 2
        send(
            val_ref.at[:, cols(to_y * 2 + to_s, 128)], vb2.at[y, k, s, x], V3,
            row_of(to_y, zh, k), ((1 - h) * 2 + to_s) * 4 + x,
        )
    sent(cb2.at[0], ssem.at[C3])
    sent(vb2.at[0, 0], ssem.at[V3])
    arrived(da, DA)
    das[...] = jnp.sum(da[...], axis=0)
    for d in (4, 5, 2, 3, 6, 7, 1):
        to_y, to_s = (y + d // 2) % 4, (s + d) % 2
        send(das, db.at[y * 2 + s], DB, row_of(to_y, zh, k), (h * 2 + to_s) * 4 + x)
    keep(das, db.at[y * 2 + s], DB)
    sent(db.at[0:7], ssem.at[DB])
    arrived(db, DB)
    dbs[...] = jnp.sum(db[...], axis=0)

    for e in range(2):
        send_or_keep(dbs, dw.at[h], rsem.at[DW], selfsem.at[1 + e], density_peer(e))
    arrived(cb2.at[y], C3)
    for d in (2, 1, 3):
        send(cb2.at[y], cb2.at[y], C4, row_of((y + d) % 4, zh, k), col)
    theirs = vb2.at[:, k, :, x]
    arrived(theirs, V3)
    for d in (4, 5, 2, 3, 6, 7, 1):
        to_x, to_k = (x + d // 2) % 4, (k + d) % 2
        send(theirs, theirs, V4, row_of(y, zh, to_k), zl * 4 + to_x)
    sent(cb2.at[0:3], ssem.at[C4])
    sent(vt.at[0:4, 0:112], ssem.at[V4])
    arrived(dw, DW)
    d0, d1 = dw[0], dw[1]
    dens = jnp.concatenate([d0[0:4], d1[0:4], d0[4:8], d1[4:8]], axis=1)
    dens = jnp.concatenate([dens, dens], axis=0)
    scr = dot3(halves(dens), (wh[...], wl[...]), NT)
    sp[...] = jnp.concatenate([scr[0:4, :128], scr[0:4, 128:]], axis=0)

    for d in (10, 6, 14, 8, 9, 11, 12, 13, 4, 5, 7, 15, 2, 1, 3):
        send(sp, sa.at[col], SA, row, (col + d) % 16)
    keep(sp, sa.at[col], SA)
    sent(sa.at[0:15], ssem.at[SA])
    arrived(cb2.at[0:3], C4)
    arrived(vt.at[0:4, 0:112], V4)
    for blk in range(4):
        ch[4 + blk], cl[4 + blk] = halves(cb2[blk].reshape(256, 128))
        vt[4 + blk] = vb2[blk].reshape(256, 128).T
    arrived(sa, SA)
    sas[...] = jnp.sum(sa[...], axis=0)
    for d in (4, 5, 2, 3, 6, 7, 1):
        to_y, to_k = (y + d // 2) % 4, (k + d) % 2
        send(sas, sb.at[y * 2 + k], SB, row_of(to_y, zh, to_k), col)
    keep(sas, sb.at[y * 2 + k], SB)
    sent(sb.at[0:7], ssem.at[SB])
    arrived(sb, SB)

    away = (s * 8 + k * 2 + x % 2 - zh * 4 - zl + 33) % 16
    far = jnp.where(away < 7, 1, 0)
    pots = []
    for blk in range(8):
        tiles = (sb[blk % 4 * 2], sb[blk % 4 * 2 + 1])
        pots.append(jnp.concatenate([jnp.where((h == 0) == (blk < 4), t[0:4], t[4:8]) for t in tiles], axis=1))
    lane = lax.broadcasted_iota(jnp.int32, (4, 16, 128), 2)
    for hold in (far, 1 - far):
        acc = jnp.zeros((256, 128), F32)
        for blk in range(8):
            rows = vt[blk, pl.ds(pl.multiple_of(hold * 64, 64), 64), :]
            weighted = (rows[None] * pots[blk][:, None, :]).reshape(256, 256)
            acc = acc + dot3(halves(weighted), (ch[blk], cl[blk]), NN)
        acc = acc.reshape(4, 4, 16, 128)
        for v in range(2):
            one, two = acc[:, v * 2], acc[:, v * 2 + 1]
            low = jnp.where(lane < 64, one, pltpu.roll(two, 64, 2))
            high = jnp.where(lane < 64, pltpu.roll(one, 64, 2), two)
            kp[hold * 2 + v] = jnp.where(h == 0, low, high)
        for j in (1, 0):
            slot = hold * 2 + (k + j) % 2
            to = pair_peer(slot * 2 + h)
            if hold is far or j:
                send(kp.at[slot], kr.at[zh], KD, *to)
            else:
                send_or_keep(kp.at[slot], kr.at[zh], rsem.at[KD], selfsem.at[3], to)
    sent(kr.at[0:3], ssem.at[KD])
    arrived(kr, KD)
    total = jnp.sum(kr[...], axis=0)
    eye = lax.broadcasted_iota(jnp.int32, (32, 32), 0) == lax.broadcasted_iota(jnp.int32, (32, 32), 1)
    ev = jnp.sum(jnp.where(eye, ev_ref[...], 0.0), axis=1, keepdims=True)
    diff = ec_ref[...] - ev
    out_ref[:, 0:16, :] = diff[None, 0:16] * xv[:, 0:16, :] + total[:, :, :64]
    out_ref[:, 16:32, :] = diff[None, 16:32] * xv[:, 16:32, :] + total[:, :, 64:]

    for wait in leaving:
        wait()


def per_device(x_pairs, eps_val, eps_con, orb_val, orb_con, screened_w):
    vmem = pl.BlockSpec(memory_space=pltpu.VMEM)
    anywhere = pl.BlockSpec(memory_space=pl.ANY)
    return pl.pallas_call(
        kernel,
        out_shape=jax.ShapeDtypeStruct((4, 32, 64), F32),
        in_specs=[anywhere, vmem, vmem, anywhere, anywhere, anywhere],
        out_specs=vmem,
        scratch_shapes=[
            pltpu.VMEM((4, 32, 64), F32),
            pltpu.VMEM((256, 512), F32),
            pltpu.VMEM((4, 16, 128), F32),
            pltpu.VMEM((8, 4, 16, 128), F32),
            pltpu.VMEM((4, 2, 2, 4, 16, 128), F32),
            pltpu.VMEM((4, 2, 2, 4, 16, 128), F32),
            pltpu.VMEM((4, 2, 2, 4, 16, 128), F32),
            pltpu.VMEM((4, 2, 2, 4, 16, 128), F32),
            pltpu.VMEM((8, 128, 256), F32),
            pltpu.VMEM((8, 256, 128), BF16),
            pltpu.VMEM((8, 256, 128), BF16),
            pltpu.VMEM((256, 512), BF16),
            pltpu.VMEM((256, 512), BF16),
            pltpu.VMEM((4, 8, 128), F32),
            pltpu.VMEM((8, 8, 128), F32),
            pltpu.VMEM((8, 128), F32),
            pltpu.VMEM((8, 8, 128), F32),
            pltpu.VMEM((8, 128), F32),
            pltpu.VMEM((2, 8, 128), F32),
            pltpu.VMEM((8, 128), F32),
            pltpu.VMEM((16, 8, 128), F32),
            pltpu.VMEM((8, 128), F32),
            pltpu.VMEM((8, 8, 128), F32),
            pltpu.VMEM((4, 4, 16, 128), F32),
            pltpu.VMEM((4, 4, 16, 128), F32),
            pltpu.SemaphoreType.DMA((NSEM,)),
            pltpu.SemaphoreType.DMA((NSEM,)),
            pltpu.SemaphoreType.DMA((4,)),
            pltpu.SemaphoreType.DMA((8,)),
            pltpu.SemaphoreType.DMA((3, 4)),
            pltpu.SemaphoreType.DMA((2,)),
            pltpu.SemaphoreType.REGULAR((1,)),
        ],
        compiler_params=pltpu.CompilerParams(has_side_effects=True, collective_id=0),
        name="bse_apply",
    )(x_pairs, eps_val[None], eps_con[None], orb_val, orb_con, screened_w)


def solution(mesh):
    in_specs = (
        P(None, "rowpt", "colpt"),
        P("rowpt"),
        P("colpt"),
        P(("rowpt", "colpt"), None),
        P(("rowpt", "colpt"), None),
        P("rowpt", "colpt"),
    )
    out_specs = P(None, "rowpt", "colpt")
    return jax.shard_map(
        per_device, mesh=mesh, in_specs=in_specs, out_specs=out_specs, check_vma=False
    )
```
